128 devices in a mesh: expert: 16 (over z_hi, x, core), dp: 8 (over z_lo, y).
Axes of the slice: x: 4, y: 4, z: 4 (z_hi: 2, z_lo: 2; z = z_hi * 2 + z_lo), core: 2. Of those that a mesh axis runs over, the one named last changes fastest.
Arguments:
- trunk: bfloat16 [3072, 4096], P(('dp', 'expert')), may hold values from -6 to 6
- w_first: bfloat16 [16, 4096, 2048], P('expert'), may hold values from -0.09375 to 0.09375
- w_second: bfloat16 [16, 2048, 1024], P('expert'), may hold values from -0.125 to 0.125
- gates: bfloat16 [16, 8, 3072], P('expert', None, 'dp'), may hold values from 0.049804688 to 1
- d_mixed: bfloat16 [3072, 8, 1024], P(('dp', 'expert')), may hold values from -6 to 6
Outputs:
- mixed: bfloat16 [3072, 8, 1024], P(('dp', 'expert'))
- d_trunk: bfloat16 [3072, 4096], P(('dp', 'expert'))
- d_gates: bfloat16 [16, 8, 3072], P('expert', None, 'dp')
- d_w_first: bfloat16 [16, 4096, 2048], P('expert', 'dp')
- d_w_second: bfloat16 [16, 2048, 1024], P('expert', 'dp')
The draws below stay inside these ranges and needn't reach their ends.
All inputs are finite; a program needn't handle non-finite values.
Results may differ from the reference program's by a relative error of at most 0.015.
Values may be sent and summed in bfloat16 or wider, within the bound.
No kernel may reach another device: no remote copies, remote signals or barrier semaphores. Data moves between devices by JAX's collectives and lax.ppermute only.
A program may use at most 128 MiB of HBM per device.

```python
import math
import jax
import jax.numpy as jnp
from jax import lax

D = 4096
H = 2048
O = 1024
TASKS = 8
EXPERTS = 16
GROUP = 384
SAMPLES = 3072
N_DP = 8


def level_of(stream_key, shape, shards, smallest, high):
    factor_of, own = 1.0, jax.random.fold_in(stream_key, 6)
    for dim, blocks in shards:
        steps = jnp.exp(jax.random.uniform(jax.random.fold_in(own, dim), (blocks,), jnp.float32, smallest / len(shards), high / len(shards)))
        factor_of = factor_of * jnp.repeat(steps, shape[dim] // blocks).reshape([-1 if axis == dim else 1 for axis in range(len(shape))])
    return factor_of


def normal_values(own_key, dims, width, bound, cuts=(), dtype=jnp.bfloat16):
    entries = width * jax.random.normal(own_key, dims, jnp.float32)
    if cuts:
        entries = entries * level_of(own_key, dims, cuts, -0.22, 0.18)
    return jnp.clip(entries, -bound, bound).astype(dtype)


def setup_inputs(seed: int = 0) -> dict:
    arg_keys = jax.random.split(jax.random.key(seed), 6)
    return {
        "trunk": normal_values(arg_keys[0], (SAMPLES, D), 1.0, 6.0, ((0, 128),)),
        "w_first": normal_values(arg_keys[1], (EXPERTS, D, H), D ** -0.5, 0.09375, ((0, 16),)),
        "w_second": normal_values(arg_keys[2], (EXPERTS, H, O), H ** -0.5, 0.125, ((0, 16),)),
        "gates": jnp.clip(jnp.exp(math.log(1.0) - 2.9996462 * jax.random.uniform(arg_keys[3], (EXPERTS, TASKS, SAMPLES), jnp.float32) ** level_of(arg_keys[3], (EXPERTS, TASKS, SAMPLES), ((0, 16), (2, 8)), -0.2, 0.2)), 0.049804688, 1.0).astype(jnp.bfloat16),
        "d_mixed": normal_values(arg_keys[4], (SAMPLES, TASKS, O), 1.0, 6.0, ((0, 128),)),
    }


def reference(trunk, w_first, w_second, gates, d_mixed):
    cot = d_mixed.astype(jnp.float32)
    trunk_blocks = trunk.astype(jnp.float32).reshape(N_DP, GROUP, D)

    def per_expert(carry, packed):
        mixed_acc, trunk_acc = carry
        first, second, gate = packed
        pre = jnp.dot(trunk, first, preferred_element_type=jnp.float32)
        hidden = jax.nn.silu(pre).astype(jnp.bfloat16)
        output = jnp.dot(hidden, second, preferred_element_type=jnp.float32).astype(jnp.bfloat16)
        weight = gate.astype(jnp.float32)
        out_f = output.astype(jnp.float32)
        mixed_acc = mixed_acc + weight.T[:, :, None] * out_f[:, None, :]
        d_output = jnp.einsum("ts,sto->so", weight, cot).astype(jnp.bfloat16)
        d_gate = jnp.einsum("sto,so->ts", cot, out_f).astype(jnp.bfloat16)
        d_hidden = lax.dot_general(d_output, second, (((1,), (1,)), ((), ())), preferred_element_type=jnp.float32)
        sig = jax.nn.sigmoid(pre)
        d_pre = (d_hidden * sig * (1.0 + pre * (1.0 - sig))).astype(jnp.bfloat16)
        trunk_acc = trunk_acc + lax.dot_general(d_pre, first, (((1,), (1,)), ((), ())), preferred_element_type=jnp.float32)
        pre_blocks = d_pre.astype(jnp.float32).reshape(N_DP, GROUP, H)
        part_first = jnp.einsum("gsd,gsh->gdh", trunk_blocks, pre_blocks).astype(jnp.bfloat16)
        part_first = lax.optimization_barrier(part_first).astype(jnp.float32)
        d_first = jnp.sum(part_first, axis=0).astype(jnp.bfloat16)
        hid_blocks = hidden.astype(jnp.float32).reshape(N_DP, GROUP, H)
        dout_blocks = d_output.astype(jnp.float32).reshape(N_DP, GROUP, O)
        part_second = jnp.einsum("gsh,gso->gho", hid_blocks, dout_blocks).astype(jnp.bfloat16)
        part_second = lax.optimization_barrier(part_second).astype(jnp.float32)
        d_second = jnp.sum(part_second, axis=0).astype(jnp.bfloat16)
        return (mixed_acc, trunk_acc), (d_gate, d_first, d_second)

    init = (jnp.zeros((SAMPLES, TASKS, O), jnp.float32), jnp.zeros((SAMPLES, D), jnp.float32))
    (mixed_acc, trunk_acc), (d_gates, d_w_first, d_w_second) = lax.scan(per_expert, init, (w_first, w_second, gates))
    return (mixed_acc.astype(jnp.bfloat16), trunk_acc.astype(jnp.bfloat16), d_gates, d_w_first, d_w_second)
```

```python
import jax
import jax.numpy as jnp
from jax import lax
from jax.sharding import PartitionSpec as P

AXES = ("expert", "dp")
BF = jnp.bfloat16
F32 = jnp.float32


def coords(i):
    e, d = divmod(i, 8)
    zl, y = divmod(d, 4)
    zh, r = divmod(e, 8)
    x, c = divmod(r, 2)
    return x, y, zh, zl, c


def index(x, y, zh, zl, c):
    return (zh * 8 + x * 2 + c) * 8 + zl * 4 + y


def swap(v, x=0, y=0, z=0, c=0):
    pairs = []
    for i in range(128):
        px, py, pzh, pzl, pc = coords(i)
        pairs.append((i, index(px ^ x, py ^ y, pzh ^ (z >> 1), pzl ^ (z & 1), pc ^ c)))
    return lax.ppermute(v, AXES, pairs)


def put(buf, block, at):
    start = tuple(at) + (0,) * (buf.ndim - len(at))
    return lax.dynamic_update_slice(buf, block, start)


def dot(a, b, dims):
    return lax.dot_general(a, b, (dims, ((), ())), preferred_element_type=F32)


def gather_zx(block, zh, zl, x):
    z_all = jnp.zeros((2, 2) + block.shape, block.dtype)
    z_all = put(z_all, block[None, None], (zl, zh))
    for k in (2, 1, 3):
        z_all = put(z_all, swap(block, z=k)[None, None], (zl ^ (k & 1), zh ^ (k >> 1)))
    out = jnp.zeros((4,) + z_all.shape, block.dtype)
    out = put(out, z_all[None], (x,))
    for k in (2, 1, 3):
        out = put(out, swap(z_all, x=k)[None], (x ^ k,))
    return out


def pick(a, i, axis):
    return lax.dynamic_index_in_dim(a, i, axis, keepdims=False)


def on_device(trunk, w_first, w_second, gates, d_mixed):
    e = lax.axis_index("expert")
    d = lax.axis_index("dp")
    zl, y = d // 4, d % 4
    zh, x, c = e // 8, (e % 8) // 2, e % 2

    own = gather_zx(trunk, zh, zl, x)
    own = own.reshape(384, 4096)
    other = swap(own, c=1)

    gate_rows = lax.all_to_all(
        gates[0].reshape(8, 16, 24).transpose(1, 0, 2), "expert", 0, 0, tiled=True
    )
    d_out_each = jnp.einsum(
        "etr,rto->ero", gate_rows, d_mixed, preferred_element_type=F32
    ).astype(BF)
    back = lax.all_to_all(d_out_each, "expert", 0, 0, tiled=True)
    back = back.reshape(2, 4, 2, 24, 1024)
    back_z = swap(back, z=1)
    pair = jnp.where(zl == 0, jnp.stack([back, back_z]), jnp.stack([back_z, back]))
    pair = pair.transpose(3, 2, 0, 1, 4, 5)
    d_output = jnp.where(c == 0, pair, pair[::-1]).reshape(768, 1024)

    cols = trunk.reshape(24, 2, 4, 512)
    t_y = [pick(cols, y ^ k, 2).reshape(24, 1024) for k in range(4)]
    t_y = jnp.stack([t_y[0]] + [swap(t_y[k], y=k) for k in (1, 2, 3)])
    wide = gather_zx(t_y, zh, zl, x)
    wide = wide.transpose(3, 0, 1, 2, 4, 5).reshape(4, 384, 1024)
    wide_other = swap(wide, c=1)

    half = lax.dynamic_slice_in_dim(w_first[0], zl * 1024, 1024, 1)
    second = w_second[0]
    second_own = lax.dynamic_slice_in_dim(second, zl * 1024, 1024, 0)
    second_far = lax.dynamic_slice_in_dim(second, (1 - zl) * 1024, 1024, 0)

    hidden, d_pre = [], []
    for j in range(2):
        w = half[:, j * 512:(j + 1) * 512]
        pre = jnp.concatenate([dot(own, w, ((1,), (0,))), dot(other, w, ((1,), (0,)))])
        sig = jax.nn.sigmoid(pre)
        hidden.append((pre * sig).astype(BF))
        d_hidden = dot(d_output, second_own[j * 512:(j + 1) * 512], ((1,), (1,)))
        d_pre.append((d_hidden * sig * (1.0 + pre * (1.0 - sig))).astype(BF))

    parts = []
    for j in range(2):
        blocks = [d_pre[j]] + [swap(d_pre[j], y=k) for k in (1, 3, 2)]
        tile = 0.0
        for k, b in zip((0, 1, 3, 2), blocks):
            tile = tile + dot(wide[k], b[:384], ((0,), (0,)))
            tile = tile + dot(wide_other[k], b[384:], ((0,), (0,)))
        tile = tile.astype(BF).reshape(2, 512, 512)
        parts.append((pick(tile, zl, 0), swap(pick(tile, 1 - zl, 0), z=1)))
    near = jnp.concatenate([p[0] for p in parts], axis=1)
    far = jnp.concatenate([p[1] for p in parts], axis=1)
    d_first = jnp.where(
        zl == 0,
        jnp.concatenate([near, far], axis=1),
        jnp.concatenate([far, near], axis=1),
    )

    d_pre = jnp.concatenate(d_pre, axis=1)
    dt_other = dot(d_pre[384:], half, ((1,), (1,))).astype(BF)
    dt = dot(d_pre[:384], half, ((1,), (1,))) + swap(dt_other, c=1).astype(F32)
    dt = dt.astype(BF).reshape(4, 96, 4096)
    total = pick(dt, x, 0).astype(F32)
    for k in (1, 3, 2):
        total = total + swap(pick(dt, x ^ k, 0), x=k).astype(F32)
    dt = total.astype(BF).reshape(4, 24, 4096)
    zz = zl * 2 + zh
    total = pick(dt, zz, 0).astype(F32)
    for k in (1, 3, 2):
        at = (zl ^ (k & 1)) * 2 + (zh ^ (k >> 1))
        total = total + swap(pick(dt, at, 0), z=k).astype(F32)
    d_trunk = total.astype(BF)

    hidden = jnp.concatenate(hidden, axis=1)
    ds = dot(hidden, d_output, ((0,), (0,))).astype(BF).reshape(4, 256, 1024)
    total = pick(ds, y, 0).astype(F32)
    for k in (1, 3, 2):
        total = total + swap(pick(ds, y ^ k, 0), y=k).astype(F32)
    d_second = total.astype(BF)

    by_z = hidden.reshape(8, 2, 48, 1024)
    mine = pick(by_z, zl, 1).reshape(384, 1024)
    theirs = swap(pick(by_z, 1 - zl, 1).reshape(384, 1024), z=1)
    output = dot(mine, second_own, ((1,), (0,))) + dot(theirs, second_far, ((1,), (0,)))
    output = output.astype(BF).reshape(2, 4, 2, 24, 1024)
    output = jnp.where(c == 0, output, output[::-1])
    output = output.transpose(2, 1, 0, 3, 4).reshape(16, 24, 1024)
    outs = lax.all_to_all(output, "expert", 0, 0, tiled=True)
    mixed = jnp.einsum(
        "etr,ero->rto", gate_rows, outs, preferred_element_type=F32
    ).astype(BF)
    d_gate = jnp.einsum(
        "rto,ero->etr", d_mixed, outs, preferred_element_type=F32
    ).astype(BF)
    d_gate = lax.all_to_all(d_gate, "expert", 0, 0, tiled=True)
    d_gate = d_gate.transpose(1, 0, 2).reshape(8, 384)
    return (mixed, d_trunk, d_gate[None], d_first[None], d_second[None])


def solution(mesh):
    in_specs = (
        P(("dp", "expert"), None),
        P("expert", None, None),
        P("expert", None, None),
        P("expert", None, "dp"),
        P(("dp", "expert"), None, None),
    )
    out_specs = (
        P(("dp", "expert"), None, None),
        P(("dp", "expert"), None),
        P("expert", None, "dp"),
        P("expert", "dp", None),
        P("expert", "dp", None),
    )
    return jax.shard_map(
        on_device, mesh=mesh, in_specs=in_specs, out_specs=out_specs, check_vma=False
    )
```

```python
import jax
import jax.numpy as jnp
from jax import lax
from jax.experimental import pallas as pl
from jax.experimental.pallas import tpu as pltpu
from jax.sharding import PartitionSpec as P

AXES = ("expert", "dp")
BF = jnp.bfloat16
F32 = jnp.float32


def coords(i):
    e, d = divmod(i, 8)
    zl, y = divmod(d, 4)
    zh, r = divmod(e, 8)
    x, c = divmod(r, 2)
    return x, y, zh, zl, c


def index(x, y, zh, zl, c):
    return (zh * 8 + x * 2 + c) * 8 + zl * 4 + y


def swap(v, y=0, z=0, c=0):
    pairs = []
    for i in range(128):
        px, py, pzh, pzl, pc = coords(i)
        pairs.append((i, index(px, py ^ y, pzh ^ (z >> 1), pzl ^ (z & 1), pc ^ c)))
    return lax.ppermute(v, AXES, pairs)


def swap_split(v, k, first):
    pairs = []
    for i in range(128):
        px, py, pzh, pzl, pc = coords(i)
        if (pc == 0) == first:
            pzh, pzl = pzh ^ (k & 1), pzl ^ (k >> 1)
        else:
            px = px ^ k
        pairs.append((i, index(px, py, pzh, pzl, pc)))
    return lax.ppermute(v, AXES, pairs)


def after(v, *others):
    return lax.optimization_barrier((v,) + others)[0]


def grid():
    return [[coords(i), i] for i in range(128)]


def groups(key, order):
    rows = {}
    for at, i in grid():
        rows.setdefault(key(*at), []).append((order(*at), i))
    return [[i for _, i in sorted(rows[k])] for k in sorted(rows)]


PLANE = groups(lambda x, y, zh, zl, c: (y, c), lambda x, y, zh, zl, c: (x, zl, zh))
RING = groups(lambda x, y, zh, zl, c: (x, zh, zl, c), lambda x, y, zh, zl, c: y)


def exchange(v, members):
    return lax.all_to_all(v, AXES, 0, 0, axis_index_groups=members, tiled=True)


def dot(a, b, dims):
    return lax.dot_general(a, b, (dims, ((), ())), preferred_element_type=F32)


def pick(a, i, axis):
    return lax.dynamic_index_in_dim(a, i, axis, keepdims=False)


def place_kernel(at, *refs):
    out = refs[4]
    for i in range(16):
        out[at[i]] = refs[i // 4][i % 4]


def place(at, lines):
    return pl.pallas_call(
        place_kernel,
        out_shape=jax.ShapeDtypeStruct((16,) + lines[0].shape[1:], lines[0].dtype),
        in_specs=[pl.BlockSpec(memory_space=pltpu.SMEM)]
        + [pl.BlockSpec(memory_space=pltpu.VMEM)] * 4,
        out_specs=pl.BlockSpec(memory_space=pltpu.VMEM),
        compiler_params=pltpu.CompilerParams(vmem_limit_bytes=16 << 20),
        cost_estimate=pl.CostEstimate(flops=0, bytes_accessed=6 << 20, transcendentals=0),
    )(at, *lines)


def gather(v, members):
    return exchange(jnp.broadcast_to(v[None], (len(members[0]),) + v.shape), members)


def on_device(trunk, w_first, w_second, gates, d_mixed):
    e = lax.axis_index("expert")
    d = lax.axis_index("dp")
    zl, y = d // 4, d % 4
    zh, x, c = e // 8, (e % 8) // 2, e % 2
    zz = zl * 2 + zh

    gate_rows = lax.all_to_all(
        gates[0].reshape(8, 16, 24).transpose(1, 0, 2), "expert", 0, 0, tiled=True
    )

    line = jnp.stack([trunk] + [swap_split(trunk, k, True) for k in (1, 2, 3)])
    far = [swap_split(line, k, False) for k in (2, 1, 3)]
    dx, dz = x ^ (jnp.arange(16) // 4), zz ^ (jnp.arange(16) % 4)
    ex, ez = x ^ (jnp.arange(16) % 4), zz ^ (jnp.arange(16) // 4)
    at = jnp.where(c == 0, dx * 4 + dz, ex * 4 + ez).astype(jnp.int32)
    own = place(at, [line, far[1], far[0], far[2]]).reshape(384, 4096)

    d_out_each = jnp.einsum(
        "etr,rto->ero", gate_rows, d_mixed, preferred_element_type=F32
    ).astype(BF)
    back = lax.all_to_all(d_out_each, "expert", 0, 0, tiled=True)

    half = lax.dynamic_slice_in_dim(w_first[0], zl * 1024, 1024, 1)
    cols = trunk.reshape(24, 2, 4, 512)
    t_y = [pick(cols, y ^ k, 2).reshape(24, 1024) for k in range(4)]
    t_y = jnp.stack([t_y[0]] + [swap(t_y[k], y=k) for k in (1, 3, 2)])

    own, back, half, t_y = lax.optimization_barrier((own, back, half, t_y))
    other = swap(own, c=1)
    back = back.reshape(2, 4, 2, 24, 1024)
    back_z = swap(back, z=1)
    wide = gather(t_y, PLANE).reshape(16, 4, 24, 1024)
    second = w_second[0]
    second_own = lax.dynamic_slice_in_dim(second, zl * 1024, 1024, 0)
    second_far = lax.dynamic_slice_in_dim(second, (1 - zl) * 1024, 1024, 0)

    def forward(rows):
        pre = dot(rows, half, ((1,), (0,)))
        sig = jax.nn.sigmoid(pre)
        slope = sig * (1.0 + pre * (1.0 - sig))
        return (pre * sig).astype(BF), slope

    def backward(d_o, slope):
        d_hidden = dot(d_o, second_own, ((1,), (1,)))
        return (d_hidden * slope).astype(BF)

    hidden_own, slope_own = forward(own)
    hidden_own, back_z, other = lax.optimization_barrier((hidden_own, back_z, other))
    pair = jnp.where(zl == 0, jnp.stack([back, back_z]), jnp.stack([back_z, back]))
    pair = pair.transpose(3, 2, 0, 1, 4, 5)
    d_output = jnp.where(c == 0, pair, pair[::-1]).reshape(768, 1024)

    d_own = backward(d_output[:384], slope_own)
    near_own = (swap(d_own, y=1), swap(d_own, y=3))
    hidden_other, slope_other = forward(other)
    d_other = backward(d_output[384:], slope_other)
    near_other = (swap(d_other, y=1), swap(d_other, y=3))

    d_other_late, *near_own = lax.optimization_barrier((d_other, *near_own))
    dt_other = dot(d_other_late, half, ((1,), (1,))).astype(BF)
    far_own = swap(near_own[1], y=1)
    hidden = jnp.concatenate([hidden_own, hidden_other])
    d_own_late, *near_other = lax.optimization_barrier((d_own, *near_other))
    dt = dot(d_own_late, half, ((1,), (1,))) + swap(dt_other, c=1).astype(F32)
    dt = dt.astype(BF)
    far_other = swap(near_other[0], y=3)

    ds = dot(hidden, d_output, ((0,), (0,))).astype(BF)
    d_second = lax.psum_scatter(
        ds, AXES, axis_index_groups=RING, scatter_dimension=0, tiled=True
    )

    by_z = hidden.reshape(8, 2, 48, 1024)
    mine = pick(by_z, zl, 1).reshape(384, 1024)
    theirs = swap(pick(by_z, 1 - zl, 1).reshape(384, 1024), z=1)
    output = dot(mine, second_own, ((1,), (0,))) + dot(theirs, second_far, ((1,), (0,)))
    output = output.astype(BF).reshape(2, 4, 2, 24, 1024)
    output = jnp.where(c == 0, output, output[::-1])
    output = output.transpose(2, 1, 0, 3, 4).reshape(16, 24, 1024)
    outs = lax.all_to_all(output, "expert", 0, 0, tiled=True)
    mixed = jnp.einsum(
        "etr,ero->rto", gate_rows, outs, preferred_element_type=F32
    ).astype(BF)
    d_gate = jnp.einsum(
        "rto,ero->etr", d_mixed, outs, preferred_element_type=F32
    ).astype(BF)

    dt = exchange(after(dt, outs).reshape(16, 24, 4096), PLANE)
    d_trunk = jnp.sum(dt, axis=0, dtype=F32).astype(BF)
    d_gate = lax.all_to_all(after(d_gate, dt), "expert", 0, 0, tiled=True)
    d_gate = d_gate.transpose(1, 0, 2).reshape(8, 384)

    wide = after(wide, *near_other)
    wide = wide.transpose(1, 0, 2, 3).reshape(1536, 1024)
    wide_other = swap(wide, c=1)
    tile = dot(wide[:1152], jnp.concatenate([d_own, *near_own]), ((0,), (0,)))
    tile = tile + dot(wide_other[:1152], jnp.concatenate([d_other, *near_other]), ((0,), (0,)))
    tile = tile + dot(wide[1152:], far_own, ((0,), (0,)))
    tile = tile + dot(wide_other[1152:], far_other, ((0,), (0,)))
    tile = tile.astype(BF).reshape(2, 512, 1024)
    far = swap(pick(tile, 1 - zl, 0), z=1)
    near = pick(tile, zl, 0)
    d_first = jnp.where(
        zl == 0,
        jnp.concatenate([near, far], axis=1),
        jnp.concatenate([far, near], axis=1),
    )
    return (mixed, d_trunk, d_gate[None], d_first[None], d_second[None])


def solution(mesh):
    in_specs = (
        P(("dp", "expert"), None),
        P("expert", None, None),
        P("expert", None, None),
        P("expert", None, "dp"),
        P(("dp", "expert"), None, None),
    )
    out_specs = (
        P(("dp", "expert"), None, None),
        P(("dp", "expert"), None),
        P("expert", None, "dp"),
        P("expert", "dp", None),
        P("expert", "dp", None),
    )
    return jax.shard_map(
        on_device, mesh=mesh, in_specs=in_specs, out_specs=out_specs, check_vma=False
    )
```

```python
import jax
import jax.numpy as jnp
from jax import lax
from jax.experimental import pallas as pl
from jax.experimental.pallas import tpu as pltpu
from jax.sharding import PartitionSpec as P

AXES = ("expert", "dp")
BF = jnp.bfloat16
F32 = jnp.float32


def coords(i):
    e, d = divmod(i, 8)
    zl, y = divmod(d, 4)
    zh, r = divmod(e, 8)
    x, c = divmod(r, 2)
    return x, y, zh, zl, c


def index(x, y, zh, zl, c):
    return (zh * 8 + x * 2 + c) * 8 + zl * 4 + y


def swap(v, y=0, z=0, c=0):
    pairs = []
    for i in range(128):
        px, py, pzh, pzl, pc = coords(i)
        pairs.append((i, index(px, py ^ y, pzh ^ (z >> 1), pzl ^ (z & 1), pc ^ c)))
    return lax.ppermute(v, AXES, pairs)


def swap_split(v, k, first):
    pairs = []
    for i in range(128):
        px, py, pzh, pzl, pc = coords(i)
        if (pc == 0) == first:
            pzh, pzl = pzh ^ (k & 1), pzl ^ (k >> 1)
        else:
            px = px ^ k
        pairs.append((i, index(px, py, pzh, pzl, pc)))
    return lax.ppermute(v, AXES, pairs)


def after(v, *others):
    return lax.optimization_barrier((v,) + others)[0]


def grid():
    return [[coords(i), i] for i in range(128)]


def groups(key, order):
    rows = {}
    for at, i in grid():
        rows.setdefault(key(*at), []).append((order(*at), i))
    return [[i for _, i in sorted(rows[k])] for k in sorted(rows)]


PLANE = groups(lambda x, y, zh, zl, c: (y, c), lambda x, y, zh, zl, c: (x, zl, zh))
LEVEL = groups(lambda x, y, zh, zl, c: y, lambda x, y, zh, zl, c: (c, x, zl, zh))
RING = groups(lambda x, y, zh, zl, c: (x, zh, zl, c), lambda x, y, zh, zl, c: y)


def exchange(v, members):
    return lax.all_to_all(v, AXES, 0, 0, axis_index_groups=members, tiled=True)


def dot(a, b, dims):
    return lax.dot_general(a, b, (dims, ((), ())), preferred_element_type=F32)


def pick(a, i, axis):
    return lax.dynamic_index_in_dim(a, i, axis, keepdims=False)


def place_kernel(at, *refs):
    out = refs[4]
    for i in range(16):
        out[at[i]] = refs[i // 4][i % 4]


def place_columns_kernel(at, *refs):
    out = refs[4]
    for i in range(16):
        for k in range(4):
            out[k, at[i]] = refs[i // 4][i % 4, k]


def place(kernel, shape, at, lines):
    return pl.pallas_call(
        kernel,
        out_shape=jax.ShapeDtypeStruct(shape, lines[0].dtype),
        in_specs=[pl.BlockSpec(memory_space=pltpu.SMEM)]
        + [pl.BlockSpec(memory_space=pltpu.VMEM)] * 4,
        out_specs=pl.BlockSpec(memory_space=pltpu.VMEM),
        compiler_params=pltpu.CompilerParams(vmem_limit_bytes=16 << 20),
        cost_estimate=pl.CostEstimate(flops=0, bytes_accessed=6 << 20, transcendentals=0),
    )(at, *lines)


def on_device(trunk, w_first, w_second, gates, d_mixed):
    e = lax.axis_index("expert")
    d = lax.axis_index("dp")
    zl, y = d // 4, d % 4
    zh, x, c = e // 8, (e % 8) // 2, e % 2
    zz = zl * 2 + zh

    gate_rows = lax.all_to_all(
        gates[0].reshape(8, 16, 24).transpose(1, 0, 2), "expert", 0, 0, tiled=True
    )

    line = jnp.stack([trunk] + [swap_split(trunk, k, True) for k in (1, 2, 3)])
    far = [swap_split(line, k, False) for k in (2, 1, 3)]
    dx, dz = x ^ (jnp.arange(16) // 4), zz ^ (jnp.arange(16) % 4)
    ex, ez = x ^ (jnp.arange(16) % 4), zz ^ (jnp.arange(16) // 4)
    at = jnp.where(c == 0, dx * 4 + dz, ex * 4 + ez).astype(jnp.int32)
    own = place(place_kernel, (16, 24, 4096), at, [line, far[1], far[0], far[2]])
    own = own.reshape(384, 4096)

    gate_order = after(gate_rows, line).reshape(2, 4, 2, 8, 24)
    gate_order = gate_order.transpose(2, 1, 0, 3, 4).reshape(16, 8, 24)
    d_out_each = jnp.einsum(
        "etr,rto->ero", gate_order, d_mixed, preferred_element_type=F32
    ).astype(BF)
    d_out_each = d_out_each.reshape(8, 1, 2, 24, 1024)
    d_out_each = jnp.broadcast_to(d_out_each, (8, 2, 2, 24, 1024)).reshape(32, 24, 1024)
    back = exchange(d_out_each, LEVEL)

    trunk, w_first, _ = lax.optimization_barrier((trunk, w_first, d_out_each))
    half = lax.dynamic_slice_in_dim(w_first[0], zl * 1024, 1024, 1)
    cols = trunk.reshape(24, 2, 4, 512)
    t_y = [pick(cols, y ^ k, 2).reshape(24, 1024) for k in range(4)]
    t_y = jnp.stack([t_y[0]] + [swap(t_y[k], y=k) for k in (1, 3, 2)])

    own, back, half, t_y = lax.optimization_barrier((own, back, half, t_y))
    other = swap(own, c=1)
    wide = jnp.stack([t_y] + [swap_split(t_y, k, True) for k in (1, 2, 3)])
    back = back.reshape(2, 384, 1024)
    d_output = jnp.where(c == 0, back, back[::-1]).reshape(768, 1024)
    second = w_second[0]
    second_own = lax.dynamic_slice_in_dim(second, zl * 1024, 1024, 0)
    second_far = lax.dynamic_slice_in_dim(second, (1 - zl) * 1024, 1024, 0)

    def forward(rows):
        pre = dot(rows, half, ((1,), (0,)))
        sig = jax.nn.sigmoid(pre)
        slope = sig * (1.0 + pre * (1.0 - sig))
        return (pre * sig).astype(BF), slope

    def backward(d_o, slope):
        d_hidden = dot(d_o, second_own, ((1,), (1,)))
        return (d_hidden * slope).astype(BF)

    hidden_own, slope_own = forward(own)
    d_own = backward(d_output[:384], slope_own)
    d_own, other, wide = lax.optimization_barrier((d_own, other, wide))
    near_own = (swap(d_own, y=1), swap(d_own, y=3))
    hidden_other, slope_other = forward(other)
    d_other = backward(d_output[384:], slope_other)
    near_other = (swap(d_other, y=1), swap(d_other, y=3))

    hidden = jnp.concatenate([hidden_own, hidden_other])
    by_z = hidden.reshape(8, 2, 48, 1024)
    mine = pick(by_z, zl, 1).reshape(384, 1024)
    theirs = swap(pick(by_z, 1 - zl, 1).reshape(384, 1024), z=1)
    mine, near_own = lax.optimization_barrier((mine, near_own))
    output = dot(mine, second_own, ((1,), (0,))) + dot(theirs, second_far, ((1,), (0,)))
    output = output.astype(BF).reshape(2, 4, 2, 24, 1024)
    output = jnp.where(c == 0, output, output[::-1])
    output = output.transpose(2, 1, 0, 3, 4).reshape(16, 24, 1024)

    d_other_late, output = lax.optimization_barrier((d_other, output))
    outs = lax.all_to_all(output, "expert", 0, 0, tiled=True)
    far_own = swap(near_own[1], y=1)
    wide_far = [swap_split(wide, k, False) for k in (2, 1, 3)]
    dt_other = dot(d_other_late, half, ((1,), (1,))).astype(BF)
    d_own_late, near_other, wide_far, hidden, outs = lax.optimization_barrier(
        (d_own, near_other, wide_far, hidden, outs)
    )
    far_other = swap(near_other[0], y=3)
    dt = dot(d_own_late, half, ((1,), (1,))) + swap(dt_other, c=1).astype(F32)
    dt = exchange(dt.astype(BF).reshape(16, 24, 4096), PLANE)
    d_trunk = jnp.sum(dt, axis=0, dtype=F32).astype(BF)
    wide = place(
        place_columns_kernel, (4, 16, 24, 1024), at,
        [wide, wide_far[1], wide_far[0], wide_far[2]],
    ).reshape(1536, 1024)
    wide_other = swap(wide, c=1)

    ds = dot(hidden, d_output, ((0,), (0,))).astype(BF)
    d_second = lax.psum_scatter(
        ds, AXES, axis_index_groups=RING, scatter_dimension=0, tiled=True
    )

    mixed = jnp.einsum(
        "etr,ero->rto", gate_rows, outs, preferred_element_type=F32
    ).astype(BF)
    d_gate = jnp.einsum(
        "rto,ero->etr", d_mixed, outs, preferred_element_type=F32
    ).astype(BF)

    d_gate = lax.all_to_all(after(d_gate, dt), "expert", 0, 0, tiled=True)
    d_gate = d_gate.transpose(1, 0, 2).reshape(8, 384)

    wide, far_own = lax.optimization_barrier((wide, far_own))
    tile = dot(wide[:1152], jnp.concatenate([d_own, *near_own]), ((0,), (0,)))
    tile = tile + dot(wide_other[:1152], jnp.concatenate([d_other, *near_other]), ((0,), (0,)))
    tile = tile + dot(wide[1152:], far_own, ((0,), (0,)))
    tile = tile + dot(wide_other[1152:], far_other, ((0,), (0,)))
    tile = tile.astype(BF).reshape(2, 512, 1024)
    far = swap(pick(tile, 1 - zl, 0), z=1)
    near = pick(tile, zl, 0)
    d_first = jnp.where(
        zl == 0,
        jnp.concatenate([near, far], axis=1),
        jnp.concatenate([far, near], axis=1),
    )
    return (mixed, d_trunk, d_gate[None], d_first[None], d_second[None])


def solution(mesh):
    in_specs = (
        P(("dp", "expert"), None),
        P("expert", None, None),
        P("expert", None, None),
        P("expert", None, "dp"),
        P(("dp", "expert"), None, None),
    )
    out_specs = (
        P(("dp", "expert"), None, None),
        P(("dp", "expert"), None),
        P("expert", None, "dp"),
        P("expert", "dp", None),
        P("expert", "dp", None),
    )
    return jax.shard_map(
        on_device, mesh=mesh, in_specs=in_specs, out_specs=out_specs, check_vma=False
    )
```

```python
import jax
import jax.numpy as jnp
from jax import lax
from jax.experimental import pallas as pl
from jax.experimental.pallas import tpu as pltpu
from jax.sharding import PartitionSpec as P

AXES = ("expert", "dp")
BF = jnp.bfloat16
F32 = jnp.float32


def coords(i):
    e, d = divmod(i, 8)
    zl, y = divmod(d, 4)
    zh, r = divmod(e, 8)
    x, c = divmod(r, 2)
    return x, y, zh, zl, c


def index(x, y, zh, zl, c):
    return (zh * 8 + x * 2 + c) * 8 + zl * 4 + y


def swap(v, y=0, z=0, c=0):
    pairs = []
    for i in range(128):
        px, py, pzh, pzl, pc = coords(i)
        pairs.append((i, index(px, py ^ y, pzh ^ (z >> 1), pzl ^ (z & 1), pc ^ c)))
    return lax.ppermute(v, AXES, pairs)


def swap_split(v, k, first):
    pairs = []
    for i in range(128):
        px, py, pzh, pzl, pc = coords(i)
        if (pc == 0) == first:
            pzh, pzl = pzh ^ (k & 1), pzl ^ (k >> 1)
        else:
            px = px ^ k
        pairs.append((i, index(px, py, pzh, pzl, pc)))
    return lax.ppermute(v, AXES, pairs)


def after(v, *others):
    return lax.optimization_barrier((v,) + others)[0]


def grid():
    return [[coords(i), i] for i in range(128)]


def groups(key, order):
    rows = {}
    for at, i in grid():
        rows.setdefault(key(*at), []).append((order(*at), i))
    return [[i for _, i in sorted(rows[k])] for k in sorted(rows)]


PLANE = groups(lambda x, y, zh, zl, c: (y, c), lambda x, y, zh, zl, c: (x, zl, zh))
LEVEL = groups(lambda x, y, zh, zl, c: y, lambda x, y, zh, zl, c: (c, x, zl, zh))
RING = groups(lambda x, y, zh, zl, c: (x, zh, zl, c), lambda x, y, zh, zl, c: y)


def exchange(v, members):
    return lax.all_to_all(v, AXES, 0, 0, axis_index_groups=members, tiled=True)


def dot(a, b, dims):
    return lax.dot_general(a, b, (dims, ((), ())), preferred_element_type=F32)


def pick(a, i, axis):
    return lax.dynamic_index_in_dim(a, i, axis, keepdims=False)


def place_kernel(at, *refs):
    out = refs[4]
    for i in range(16):
        out[at[i]] = refs[i // 4][i % 4]


def place(kernel, shape, at, lines):
    return pl.pallas_call(
        kernel,
        out_shape=jax.ShapeDtypeStruct(shape, lines[0].dtype),
        in_specs=[pl.BlockSpec(memory_space=pltpu.SMEM)]
        + [pl.BlockSpec(memory_space=pltpu.VMEM)] * 4,
        out_specs=pl.BlockSpec(memory_space=pltpu.VMEM),
        compiler_params=pltpu.CompilerParams(vmem_limit_bytes=16 << 20),
        cost_estimate=pl.CostEstimate(flops=0, bytes_accessed=6 << 20, transcendentals=0),
    )(at, *lines)


def on_device(trunk, w_first, w_second, gates, d_mixed):
    e = lax.axis_index("expert")
    d = lax.axis_index("dp")
    zl, y = d // 4, d % 4
    zh, x, c = e // 8, (e % 8) // 2, e % 2
    zz = zl * 2 + zh

    gate_rows = lax.all_to_all(
        gates[0].reshape(8, 16, 24).transpose(1, 0, 2), "expert", 0, 0, tiled=True
    )

    line = jnp.stack([trunk] + [swap_split(trunk, k, True) for k in (1, 2, 3)])
    far = [swap_split(line, k, False) for k in (2, 1, 3)]
    dx, dz = x ^ (jnp.arange(16) // 4), zz ^ (jnp.arange(16) % 4)
    ex, ez = x ^ (jnp.arange(16) % 4), zz ^ (jnp.arange(16) // 4)
    at = jnp.where(c == 0, dx * 4 + dz, ex * 4 + ez).astype(jnp.int32)
    own = place(place_kernel, (16, 24, 4096), at, [line, far[1], far[0], far[2]])
    own = own.reshape(384, 4096)

    gate_order = after(gate_rows, line).reshape(2, 4, 2, 8, 24)
    gate_order = gate_order.transpose(2, 1, 0, 3, 4).reshape(16, 8, 24)
    d_out_each = jnp.einsum(
        "etr,rto->ero", gate_order, d_mixed, preferred_element_type=F32
    ).astype(BF)
    d_out_each = d_out_each.reshape(8, 1, 2, 24, 1024)
    d_out_each = jnp.broadcast_to(d_out_each, (8, 2, 2, 24, 1024)).reshape(32, 24, 1024)
    back = exchange(d_out_each, LEVEL)

    trunk, _ = lax.optimization_barrier((trunk, d_out_each))
    half = lax.dynamic_slice_in_dim(w_first[0], zl * 1024, 1024, 1)
    cols = trunk.reshape(24, 2, 4, 512)
    t_y = [pick(cols, y ^ k, 2).reshape(24, 1024) for k in range(4)]
    t_y = jnp.stack([t_y[0]] + [swap(t_y[k], y=k) for k in (1, 3, 2)])

    wide = lax.all_gather(t_y, AXES, axis_index_groups=PLANE, axis=0, tiled=False)
    own, back, t_y = lax.optimization_barrier((own, back, t_y))
    other = swap(own, c=1)
    back = back.reshape(2, 384, 1024)
    d_output = jnp.where(c == 0, back, back[::-1]).reshape(768, 1024)
    second = w_second[0]
    second_own = lax.dynamic_slice_in_dim(second, zl * 1024, 1024, 0)
    second_far = lax.dynamic_slice_in_dim(second, (1 - zl) * 1024, 1024, 0)

    def forward(rows):
        pre = dot(rows, half, ((1,), (0,)))
        sig = jax.nn.sigmoid(pre)
        slope = sig * (1.0 + pre * (1.0 - sig))
        return (pre * sig).astype(BF), slope

    def backward(d_o, slope):
        d_hidden = dot(d_o, second_own, ((1,), (1,)))
        return (d_hidden * slope).astype(BF)

    hidden_own, slope_own = forward(own)
    d_own = backward(d_output[:384], slope_own)
    d_own, other = lax.optimization_barrier((d_own, other))
    near_own = (swap(d_own, y=1), swap(d_own, y=3))
    hidden_other, slope_other = forward(other)
    d_other = backward(d_output[384:], slope_other)
    near_other = (swap(d_other, y=1), swap(d_other, y=3))

    hidden = jnp.concatenate([hidden_own, hidden_other])
    by_z = hidden.reshape(8, 2, 48, 1024)
    mine = pick(by_z, zl, 1).reshape(384, 1024)
    theirs = swap(pick(by_z, 1 - zl, 1).reshape(384, 1024), z=1)
    mine, near_own = lax.optimization_barrier((mine, near_own))
    output = dot(mine, second_own, ((1,), (0,))) + dot(theirs, second_far, ((1,), (0,)))
    output = output.astype(BF).reshape(2, 4, 2, 24, 1024)
    output = jnp.where(c == 0, output, output[::-1])
    output = output.transpose(2, 1, 0, 3, 4).reshape(16, 24, 1024)

    outs = lax.all_to_all(output, "expert", 0, 0, tiled=True)
    d_other_late, outs, near_other = lax.optimization_barrier((d_other, outs, near_other))
    far_own = swap(near_own[1], y=1)
    dt_other = dot(d_other_late, half, ((1,), (1,))).astype(BF)
    far_other = swap(near_other[0], y=3)
    dt = dot(d_own, half, ((1,), (1,))) + swap(dt_other, c=1).astype(F32)
    dt = exchange(dt.astype(BF).reshape(16, 24, 4096), PLANE)
    d_trunk = jnp.sum(dt, axis=0, dtype=F32).astype(BF)
    wide = after(wide, near_other[0]).transpose(1, 0, 2, 3).reshape(1536, 1024)
    wide_other = swap(wide, c=1)

    ds = dot(hidden, d_output, ((0,), (0,))).astype(BF)
    d_second = lax.psum_scatter(
        ds, AXES, axis_index_groups=RING, scatter_dimension=0, tiled=True
    )

    mixed = jnp.einsum(
        "etr,ero->rto", gate_rows, outs, preferred_element_type=F32
    ).astype(BF)
    d_gate = jnp.einsum(
        "rto,ero->etr", d_mixed, outs, preferred_element_type=F32
    ).astype(BF)

    d_gate = lax.all_to_all(after(d_gate, dt), "expert", 0, 0, tiled=True)
    d_gate = d_gate.transpose(1, 0, 2).reshape(8, 384)

    tile = dot(wide[:1152], jnp.concatenate([d_own, *near_own]), ((0,), (0,)))
    tile = tile + dot(wide_other[:1152], jnp.concatenate([d_other, *near_other]), ((0,), (0,)))
    tile = tile + dot(wide[1152:], far_own, ((0,), (0,)))
    tile = tile + dot(wide_other[1152:], far_other, ((0,), (0,)))
    tile = tile.astype(BF).reshape(2, 512, 1024)
    far = swap(pick(tile, 1 - zl, 0), z=1)
    near = pick(tile, zl, 0)
    d_first = jnp.where(
        zl == 0,
        jnp.concatenate([near, far], axis=1),
        jnp.concatenate([far, near], axis=1),
    )
    return (mixed, d_trunk, d_gate[None], d_first[None], d_second[None])


def solution(mesh):
    in_specs = (
        P(("dp", "expert"), None),
        P("expert", None, None),
        P("expert", None, None),
        P("expert", None, "dp"),
        P(("dp", "expert"), None, None),
    )
    out_specs = (
        P(("dp", "expert"), None, None),
        P(("dp", "expert"), None),
        P("expert", None, "dp"),
        P("expert", "dp", None),
        P("expert", "dp", None),
    )
    return jax.shard_map(
        on_device, mesh=mesh, in_specs=in_specs, out_specs=out_specs, check_vma=False
    )
```

```python
import jax
import jax.numpy as jnp
from jax import lax
from jax.experimental import pallas as pl
from jax.experimental.pallas import tpu as pltpu
from jax.sharding import PartitionSpec as P

AXES = ("expert", "dp")
BF = jnp.bfloat16
F32 = jnp.float32


def coords(i):
    e, d = divmod(i, 8)
    zl, y = divmod(d, 4)
    zh, r = divmod(e, 8)
    x, c = divmod(r, 2)
    return x, y, zh, zl, c


def index(x, y, zh, zl, c):
    return (zh * 8 + x * 2 + c) * 8 + zl * 4 + y


def swap(v, y=0, z=0, c=0):
    pairs = []
    for i in range(128):
        px, py, pzh, pzl, pc = coords(i)
        pairs.append((i, index(px, py ^ y, pzh ^ (z >> 1), pzl ^ (z & 1), pc ^ c)))
    return lax.ppermute(v, AXES, pairs)


def swap_split(v, k, first):
    pairs = []
    for i in range(128):
        px, py, pzh, pzl, pc = coords(i)
        if (pc == 0) == first:
            pzh, pzl = pzh ^ (k & 1), pzl ^ (k >> 1)
        else:
            px = px ^ k
        pairs.append((i, index(px, py, pzh, pzl, pc)))
    return lax.ppermute(v, AXES, pairs)


def after(v, *others):
    return lax.optimization_barrier((v,) + others)[0]


def grid():
    return [[coords(i), i] for i in range(128)]


def groups(key, order):
    rows = {}
    for at, i in grid():
        rows.setdefault(key(*at), []).append((order(*at), i))
    return [[i for _, i in sorted(rows[k])] for k in sorted(rows)]


PLANE = groups(lambda x, y, zh, zl, c: (y, c), lambda x, y, zh, zl, c: (x, zl, zh))
RING = groups(lambda x, y, zh, zl, c: (x, zh, zl, c), lambda x, y, zh, zl, c: y)


def exchange(v, members):
    return lax.all_to_all(v, AXES, 0, 0, axis_index_groups=members, tiled=True)


def dot(a, b, dims):
    return lax.dot_general(a, b, (dims, ((), ())), preferred_element_type=F32)


def pick(a, i, axis):
    return lax.dynamic_index_in_dim(a, i, axis, keepdims=False)


def gather(v, members):
    return exchange(jnp.broadcast_to(v[None], (len(members[0]),) + v.shape), members)


def place_kernel(at, *refs):
    out = refs[4]
    for i in range(16):
        out[at[i]] = refs[i // 4][i % 4]


def place(kernel, shape, at, lines):
    return pl.pallas_call(
        kernel,
        out_shape=jax.ShapeDtypeStruct(shape, lines[0].dtype),
        in_specs=[pl.BlockSpec(memory_space=pltpu.SMEM)]
        + [pl.BlockSpec(memory_space=pltpu.VMEM)] * 4,
        out_specs=pl.BlockSpec(memory_space=pltpu.VMEM),
        compiler_params=pltpu.CompilerParams(vmem_limit_bytes=16 << 20),
        cost_estimate=pl.CostEstimate(flops=0, bytes_accessed=6 << 20, transcendentals=0),
    )(at, *lines)


def on_device(trunk, w_first, w_second, gates, d_mixed):
    e = lax.axis_index("expert")
    d = lax.axis_index("dp")
    zl, y = d // 4, d % 4
    zh, x, c = e // 8, (e % 8) // 2, e % 2
    zz = zl * 2 + zh

    gate_rows = lax.all_to_all(
        gates[0].reshape(8, 16, 24).transpose(1, 0, 2), "expert", 0, 0, tiled=True
    )

    line = jnp.stack([trunk] + [swap_split(trunk, k, True) for k in (1, 2, 3)])
    far = [swap_split(line, k, False) for k in (2, 1, 3)]
    dx, dz = x ^ (jnp.arange(16) // 4), zz ^ (jnp.arange(16) % 4)
    ex, ez = x ^ (jnp.arange(16) % 4), zz ^ (jnp.arange(16) // 4)
    at = jnp.where(c == 0, dx * 4 + dz, ex * 4 + ez).astype(jnp.int32)
    own = place(place_kernel, (16, 24, 4096), at, [line, far[1], far[0], far[2]])
    own = own.reshape(384, 4096)

    d_out_each = jnp.einsum(
        "etr,rto->ero", after(gate_rows, line), d_mixed, preferred_element_type=F32
    ).astype(BF)
    back = lax.all_to_all(d_out_each, "expert", 0, 0, tiled=True)

    trunk, _ = lax.optimization_barrier((trunk, d_out_each))
    half = lax.dynamic_slice_in_dim(w_first[0], zl * 1024, 1024, 1)
    cols = trunk.reshape(24, 2, 4, 512)
    t_y = [pick(cols, y ^ k, 2).reshape(24, 1024) for k in range(4)]
    t_y = jnp.stack([t_y[0]] + [swap(t_y[k], y=k) for k in (1, 3, 2)])

    own, back, t_y = lax.optimization_barrier((own, back, t_y))
    other = swap(own, c=1)
    back = back.reshape(2, 4, 2, 24, 1024)
    back_z = swap(back, z=1)

    second = w_second[0]
    second_own = lax.dynamic_slice_in_dim(second, zl * 1024, 1024, 0)
    second_far = lax.dynamic_slice_in_dim(second, (1 - zl) * 1024, 1024, 0)

    def forward(rows):
        pre = dot(rows, half, ((1,), (0,)))
        sig = jax.nn.sigmoid(pre)
        slope = sig * (1.0 + pre * (1.0 - sig))
        return (pre * sig).astype(BF), slope

    def backward(d_o, slope):
        d_hidden = dot(d_o, second_own, ((1,), (1,)))
        return (d_hidden * slope).astype(BF)

    hidden_own, slope_own = forward(own)
    hidden_own, back_z, t_y = lax.optimization_barrier((hidden_own, back_z, t_y))
    wide = gather(t_y, PLANE)
    pair = jnp.where(zl == 0, jnp.stack([back, back_z]), jnp.stack([back_z, back]))
    pair = pair.transpose(3, 2, 0, 1, 4, 5)
    d_output = jnp.where(c == 0, pair, pair[::-1]).reshape(768, 1024)

    d_own = backward(d_output[:384], slope_own)
    d_own, other = lax.optimization_barrier((d_own, other))
    near_own = (swap(d_own, y=1), swap(d_own, y=3))
    hidden_other, slope_other = forward(other)
    d_other = backward(d_output[384:], slope_other)
    near_other = (swap(d_other, y=1), swap(d_other, y=3))
    hidden = jnp.concatenate([hidden_own, hidden_other])
    by_z = hidden.reshape(8, 2, 48, 1024)
    mine = pick(by_z, zl, 1).reshape(384, 1024)
    theirs = swap(pick(by_z, 1 - zl, 1).reshape(384, 1024), z=1)

    d_late, near_own = lax.optimization_barrier((d_other, near_own))
    far_own = swap(near_own[1], y=1)
    dt_other = dot(d_late, half, ((1,), (1,))).astype(BF)
    dt = dot(d_own, half, ((1,), (1,))) + swap(dt_other, c=1).astype(F32)
    dt = dt.astype(BF)

    dt, mine, near_other, wide = lax.optimization_barrier((dt, mine, near_other, wide))
    far_other = swap(near_other[0], y=3)
    output = dot(mine, second_own, ((1,), (0,))) + dot(theirs, second_far, ((1,), (0,)))
    output = output.astype(BF).reshape(2, 4, 2, 24, 1024)
    output = jnp.where(c == 0, output, output[::-1])
    output = output.transpose(2, 1, 0, 3, 4).reshape(16, 24, 1024)
    outs = lax.all_to_all(output, "expert", 0, 0, tiled=True)
    dt, outs, far_own = lax.optimization_barrier((dt, outs, far_own))
    dt = exchange(dt.reshape(16, 24, 4096), PLANE)
    d_trunk = jnp.sum(dt, axis=0, dtype=F32).astype(BF)
    wide = wide.reshape(16, 4, 24, 1024).transpose(1, 0, 2, 3).reshape(1536, 1024)
    wide_other = swap(wide, c=1)

    ds = dot(hidden, d_output, ((0,), (0,))).astype(BF)
    d_second = lax.psum_scatter(
        ds, AXES, axis_index_groups=RING, scatter_dimension=0, tiled=True
    )

    mixed = jnp.einsum(
        "etr,ero->rto", gate_rows, outs, preferred_element_type=F32
    ).astype(BF)
    d_gate = jnp.einsum(
        "rto,ero->etr", d_mixed, outs, preferred_element_type=F32
    ).astype(BF)

    d_gate = lax.all_to_all(after(d_gate, dt), "expert", 0, 0, tiled=True)
    d_gate = d_gate.transpose(1, 0, 2).reshape(8, 384)

    tile = dot(wide[:1152], jnp.concatenate([d_own, *near_own]), ((0,), (0,)))
    tile = tile + dot(wide_other[:1152], jnp.concatenate([d_other, *near_other]), ((0,), (0,)))
    tile = tile + dot(wide[1152:], far_own, ((0,), (0,)))
    tile = tile + dot(wide_other[1152:], far_other, ((0,), (0,)))
    tile = tile.astype(BF).reshape(2, 512, 1024)
    far = swap(pick(tile, 1 - zl, 0), z=1)
    near = pick(tile, zl, 0)
    d_first = jnp.where(
        zl == 0,
        jnp.concatenate([near, far], axis=1),
        jnp.concatenate([far, near], axis=1),
    )
    return (mixed, d_trunk, d_gate[None], d_first[None], d_second[None])


def solution(mesh):
    in_specs = (
        P(("dp", "expert"), None),
        P("expert", None, None),
        P("expert", None, None),
        P("expert", None, "dp"),
        P(("dp", "expert"), None, None),
    )
    out_specs = (
        P(("dp", "expert"), None, None),
        P(("dp", "expert"), None),
        P("expert", None, "dp"),
        P("expert", "dp", None),
        P("expert", "dp", None),
    )
    return jax.shard_map(
        on_device, mesh=mesh, in_specs=in_specs, out_specs=out_specs, check_vma=False
    )
```

```python
import jax
import jax.numpy as jnp
from jax import lax
from jax.experimental import pallas as pl
from jax.experimental.pallas import tpu as pltpu
from jax.sharding import PartitionSpec as P

AXES = ("expert", "dp")
BF = jnp.bfloat16
F32 = jnp.float32


def coords(i):
    e, d = divmod(i, 8)
    zl, y = divmod(d, 4)
    zh, r = divmod(e, 8)
    x, c = divmod(r, 2)
    return x, y, zh, zl, c


def index(x, y, zh, zl, c):
    return (zh * 8 + x * 2 + c) * 8 + zl * 4 + y


def swap(v, y=0, z=0, c=0):
    pairs = []
    for i in range(128):
        px, py, pzh, pzl, pc = coords(i)
        pairs.append((i, index(px, py ^ y, pzh ^ (z >> 1), pzl ^ (z & 1), pc ^ c)))
    return lax.ppermute(v, AXES, pairs)


def swap_split(v, k, first):
    pairs = []
    for i in range(128):
        px, py, pzh, pzl, pc = coords(i)
        if (pc == 0) == first:
            pzh, pzl = pzh ^ (k & 1), pzl ^ (k >> 1)
        else:
            px = px ^ k
        pairs.append((i, index(px, py, pzh, pzl, pc)))
    return lax.ppermute(v, AXES, pairs)


def after(v, *others):
    return lax.optimization_barrier((v,) + others)[0]


def grid():
    return [[coords(i), i] for i in range(128)]


def groups(key, order):
    rows = {}
    for at, i in grid():
        rows.setdefault(key(*at), []).append((order(*at), i))
    return [[i for _, i in sorted(rows[k])] for k in sorted(rows)]


PLANE = groups(lambda x, y, zh, zl, c: (y, c), lambda x, y, zh, zl, c: (x, zl, zh))
RING = groups(lambda x, y, zh, zl, c: (x, zh, zl, c), lambda x, y, zh, zl, c: y)


def exchange(v, members):
    return lax.all_to_all(v, AXES, 0, 0, axis_index_groups=members, tiled=True)


def dot(a, b, dims):
    return lax.dot_general(a, b, (dims, ((), ())), preferred_element_type=F32)


def pick(a, i, axis):
    return lax.dynamic_index_in_dim(a, i, axis, keepdims=False)


def gather(v, members):
    return exchange(jnp.broadcast_to(v[None], (len(members[0]),) + v.shape), members)


def place_kernel(at, *refs):
    out = refs[4]
    for i in range(16):
        out[at[i]] = refs[i // 4][i % 4]


def place(kernel, shape, at, lines):
    return pl.pallas_call(
        kernel,
        out_shape=jax.ShapeDtypeStruct(shape, lines[0].dtype),
        in_specs=[pl.BlockSpec(memory_space=pltpu.SMEM)]
        + [pl.BlockSpec(memory_space=pltpu.VMEM)] * 4,
        out_specs=pl.BlockSpec(memory_space=pltpu.VMEM),
        compiler_params=pltpu.CompilerParams(vmem_limit_bytes=16 << 20),
        cost_estimate=pl.CostEstimate(flops=0, bytes_accessed=6 << 20, transcendentals=0),
    )(at, *lines)


def on_device(trunk, w_first, w_second, gates, d_mixed):
    e = lax.axis_index("expert")
    d = lax.axis_index("dp")
    zl, y = d // 4, d % 4
    zh, x, c = e // 8, (e % 8) // 2, e % 2
    zz = zl * 2 + zh

    gate_rows = lax.all_to_all(
        gates[0].reshape(8, 16, 24).transpose(1, 0, 2), "expert", 0, 0, tiled=True
    )

    line = jnp.stack([trunk] + [swap_split(trunk, k, True) for k in (1, 2, 3)])
    far = [swap_split(line, k, False) for k in (2, 1, 3)]
    dx, dz = x ^ (jnp.arange(16) // 4), zz ^ (jnp.arange(16) % 4)
    ex, ez = x ^ (jnp.arange(16) % 4), zz ^ (jnp.arange(16) // 4)
    at = jnp.where(c == 0, dx * 4 + dz, ex * 4 + ez).astype(jnp.int32)
    own = place(place_kernel, (16, 24, 4096), at, [line, far[1], far[0], far[2]])
    own = own.reshape(384, 4096)

    d_out_each = jnp.einsum(
        "etr,rto->ero", after(gate_rows, line), d_mixed, preferred_element_type=F32
    ).astype(BF)
    back = lax.all_to_all(d_out_each, "expert", 0, 0, tiled=True)

    trunk, _ = lax.optimization_barrier((trunk, d_out_each))
    half = lax.dynamic_slice_in_dim(w_first[0], zl * 1024, 1024, 1)
    cols = trunk.reshape(24, 2, 4, 512)
    t_y = [pick(cols, y ^ k, 2).reshape(24, 1024) for k in range(4)]
    t_y = jnp.stack([t_y[0]] + [swap(t_y[k], y=k) for k in (1, 3, 2)])

    own, back, t_y = lax.optimization_barrier((own, back, t_y))
    other = swap(own, c=1)
    back = back.reshape(2, 4, 2, 24, 1024)
    back_z = swap(back, z=1)

    second = w_second[0]
    second_own = lax.dynamic_slice_in_dim(second, zl * 1024, 1024, 0)
    second_far = lax.dynamic_slice_in_dim(second, (1 - zl) * 1024, 1024, 0)

    def forward(rows):
        pre = dot(rows, half, ((1,), (0,)))
        sig = jax.nn.sigmoid(pre)
        slope = sig * (1.0 + pre * (1.0 - sig))
        return (pre * sig).astype(BF), slope

    def backward(d_o, slope):
        d_hidden = dot(d_o, second_own, ((1,), (1,)))
        return (d_hidden * slope).astype(BF)

    hidden_own, slope_own = forward(own)
    hidden_own, back_z, t_y = lax.optimization_barrier((hidden_own, back_z, t_y))
    wide = gather(t_y, PLANE)
    pair = jnp.where(zl == 0, jnp.stack([back, back_z]), jnp.stack([back_z, back]))
    pair = pair.transpose(3, 2, 0, 1, 4, 5)
    d_output = jnp.where(c == 0, pair, pair[::-1]).reshape(768, 1024)

    d_own = backward(d_output[:384], slope_own)
    d_own, other = lax.optimization_barrier((d_own, other))
    near_own = (swap(d_own, y=1), swap(d_own, y=3))
    hidden_other, slope_other = forward(other)
    d_other = backward(d_output[384:], slope_other)
    near_other = (swap(d_other, y=1), swap(d_other, y=3))
    hidden = jnp.concatenate([hidden_own, hidden_other])
    by_z = hidden.reshape(8, 2, 48, 1024)
    mine = pick(by_z, zl, 1).reshape(384, 1024)
    theirs = swap(pick(by_z, 1 - zl, 1).reshape(384, 1024), z=1)

    d_late, near_own = lax.optimization_barrier((d_other, near_own))
    far_own = swap(near_own[1], y=1)
    dt_other = dot(d_late, half, ((1,), (1,))).astype(BF)

    mine, theirs, near_other, wide, dt_other = lax.optimization_barrier(
        (mine, theirs, near_other, wide, dt_other)
    )
    far_other = swap(near_other[0], y=3)
    output = dot(mine, second_own, ((1,), (0,))) + dot(theirs, second_far, ((1,), (0,)))
    output = output.astype(BF).reshape(2, 4, 2, 24, 1024)
    output = jnp.where(c == 0, output, output[::-1])
    output = output.transpose(2, 1, 0, 3, 4).reshape(16, 24, 1024)
    outs = lax.all_to_all(output, "expert", 0, 0, tiled=True)
    dt = dot(after(d_own, output), half, ((1,), (1,))) + swap(dt_other, c=1).astype(F32)
    dt = dt.astype(BF)
    dt, outs, far_own = lax.optimization_barrier((dt, outs, far_own))
    dt = exchange(dt.reshape(16, 24, 4096), PLANE)
    d_trunk = jnp.sum(dt, axis=0, dtype=F32).astype(BF)
    wide = wide.reshape(16, 4, 24, 1024).transpose(1, 0, 2, 3).reshape(1536, 1024)
    wide_other = swap(wide, c=1)

    ds = dot(hidden, d_output, ((0,), (0,))).astype(BF)
    d_second = lax.psum_scatter(
        ds, AXES, axis_index_groups=RING, scatter_dimension=0, tiled=True
    )

    mixed = jnp.einsum(
        "etr,ero->rto", gate_rows, outs, preferred_element_type=F32
    ).astype(BF)
    d_gate = jnp.einsum(
        "rto,ero->etr", d_mixed, outs, preferred_element_type=F32
    ).astype(BF)

    d_gate = lax.all_to_all(after(d_gate, dt), "expert", 0, 0, tiled=True)
    d_gate = d_gate.transpose(1, 0, 2).reshape(8, 384)

    tile = dot(wide[:1152], jnp.concatenate([d_own, *near_own]), ((0,), (0,)))
    tile = tile + dot(wide_other[:1152], jnp.concatenate([d_other, *near_other]), ((0,), (0,)))
    tile = tile + dot(wide[1152:], far_own, ((0,), (0,)))
    tile = tile + dot(wide_other[1152:], far_other, ((0,), (0,)))
    tile = tile.astype(BF).reshape(2, 512, 1024)
    far = swap(pick(tile, 1 - zl, 0), z=1)
    near = pick(tile, zl, 0)
    d_first = jnp.where(
        zl == 0,
        jnp.concatenate([near, far], axis=1),
        jnp.concatenate([far, near], axis=1),
    )
    return (mixed, d_trunk, d_gate[None], d_first[None], d_second[None])


def solution(mesh):
    in_specs = (
        P(("dp", "expert"), None),
        P("expert", None, None),
        P("expert", None, None),
        P("expert", None, "dp"),
        P(("dp", "expert"), None, None),
    )
    out_specs = (
        P(("dp", "expert"), None, None),
        P(("dp", "expert"), None),
        P("expert", None, "dp"),
        P("expert", "dp", None),
        P("expert", "dp", None),
    )
    return jax.shard_map(
        on_device, mesh=mesh, in_specs=in_specs, out_specs=out_specs, check_vma=False
    )
```

```python
import jax
import jax.numpy as jnp
from jax import lax
from jax.experimental import pallas as pl
from jax.experimental.pallas import tpu as pltpu
from jax.sharding import PartitionSpec as P

AXES = ("expert", "dp")
BF = jnp.bfloat16
F32 = jnp.float32


def coords(i):
    e, d = divmod(i, 8)
    zl, y = divmod(d, 4)
    zh, r = divmod(e, 8)
    x, c = divmod(r, 2)
    return x, y, zh, zl, c


def index(x, y, zh, zl, c):
    return (zh * 8 + x * 2 + c) * 8 + zl * 4 + y


def swap(v, y=0, z=0, c=0):
    pairs = []
    for i in range(128):
        px, py, pzh, pzl, pc = coords(i)
        pairs.append((i, index(px, py ^ y, pzh ^ (z >> 1), pzl ^ (z & 1), pc ^ c)))
    return lax.ppermute(v, AXES, pairs)


def swap_split(v, k, first):
    pairs = []
    for i in range(128):
        px, py, pzh, pzl, pc = coords(i)
        if (pc == 0) == first:
            pzh, pzl = pzh ^ (k & 1), pzl ^ (k >> 1)
        else:
            px = px ^ k
        pairs.append((i, index(px, py, pzh, pzl, pc)))
    return lax.ppermute(v, AXES, pairs)


def after(v, *others):
    return lax.optimization_barrier((v,) + others)[0]


def grid():
    return [[coords(i), i] for i in range(128)]


def groups(key, order):
    rows = {}
    for at, i in grid():
        rows.setdefault(key(*at), []).append((order(*at), i))
    return [[i for _, i in sorted(rows[k])] for k in sorted(rows)]


PLANE = groups(lambda x, y, zh, zl, c: (y, c), lambda x, y, zh, zl, c: (x, zl, zh))
RING = groups(lambda x, y, zh, zl, c: (x, zh, zl, c), lambda x, y, zh, zl, c: y)


def exchange(v, members):
    return lax.all_to_all(v, AXES, 0, 0, axis_index_groups=members, tiled=True)


def dot(a, b, dims):
    return lax.dot_general(a, b, (dims, ((), ())), preferred_element_type=F32)


def pick(a, i, axis):
    return lax.dynamic_index_in_dim(a, i, axis, keepdims=False)


def gather(v, members):
    return exchange(jnp.broadcast_to(v[None], (len(members[0]),) + v.shape), members)


def place_kernel(at, *refs):
    out = refs[4]
    for i in range(16):
        out[at[i]] = refs[i // 4][i % 4]


def place(kernel, shape, at, lines):
    return pl.pallas_call(
        kernel,
        out_shape=jax.ShapeDtypeStruct(shape, lines[0].dtype),
        in_specs=[pl.BlockSpec(memory_space=pltpu.SMEM)]
        + [pl.BlockSpec(memory_space=pltpu.VMEM)] * 4,
        out_specs=pl.BlockSpec(memory_space=pltpu.VMEM),
        compiler_params=pltpu.CompilerParams(vmem_limit_bytes=16 << 20),
        cost_estimate=pl.CostEstimate(flops=0, bytes_accessed=6 << 20, transcendentals=0),
    )(at, *lines)


def on_device(trunk, w_first, w_second, gates, d_mixed):
    e = lax.axis_index("expert")
    d = lax.axis_index("dp")
    zl, y = d // 4, d % 4
    zh, x, c = e // 8, (e % 8) // 2, e % 2
    zz = zl * 2 + zh

    gate_rows = lax.all_to_all(
        gates[0].reshape(8, 16, 24).transpose(1, 0, 2), "expert", 0, 0, tiled=True
    )

    line = jnp.stack([trunk] + [swap_split(trunk, k, True) for k in (1, 2, 3)])
    far = [swap_split(line, k, False) for k in (2, 1, 3)]
    dx, dz = x ^ (jnp.arange(16) // 4), zz ^ (jnp.arange(16) % 4)
    ex, ez = x ^ (jnp.arange(16) % 4), zz ^ (jnp.arange(16) // 4)
    at = jnp.where(c == 0, dx * 4 + dz, ex * 4 + ez).astype(jnp.int32)
    own = place(place_kernel, (16, 24, 4096), at, [line, far[1], far[0], far[2]])
    own = own.reshape(384, 4096)

    d_out_each = jnp.einsum(
        "etr,rto->ero", after(gate_rows, line), d_mixed, preferred_element_type=F32
    ).astype(BF)
    back = lax.all_to_all(d_out_each, "expert", 0, 0, tiled=True)

    trunk, _ = lax.optimization_barrier((trunk, d_out_each))
    half = lax.dynamic_slice_in_dim(w_first[0], zl * 1024, 1024, 1)
    cols = trunk.reshape(24, 2, 4, 512)
    t_y = [pick(cols, y ^ k, 2).reshape(24, 1024) for k in range(4)]
    t_y = jnp.stack([t_y[0]] + [swap(t_y[k], y=k) for k in (1, 3, 2)])

    own, back, t_y = lax.optimization_barrier((own, back, t_y))
    other = swap(own, c=1)
    back = back.reshape(2, 4, 2, 24, 1024)
    back_z = swap(back, z=1)

    second = w_second[0]
    second_own = lax.dynamic_slice_in_dim(second, zl * 1024, 1024, 0)
    second_far = lax.dynamic_slice_in_dim(second, (1 - zl) * 1024, 1024, 0)

    def forward(rows):
        pre = dot(rows, half, ((1,), (0,)))
        sig = jax.nn.sigmoid(pre)
        slope = sig * (1.0 + pre * (1.0 - sig))
        return (pre * sig).astype(BF), slope

    def backward(d_o, slope):
        d_hidden = dot(d_o, second_own, ((1,), (1,)))
        return (d_hidden * slope).astype(BF)

    hidden_own, slope_own = forward(own)
    hidden_own, back_z = lax.optimization_barrier((hidden_own, back_z))
    pair = jnp.where(zl == 0, jnp.stack([back, back_z]), jnp.stack([back_z, back]))
    pair = pair.transpose(3, 2, 0, 1, 4, 5)
    d_output = jnp.where(c == 0, pair, pair[::-1]).reshape(768, 1024)

    d_own = backward(d_output[:384], slope_own)
    d_own, other, t_y = lax.optimization_barrier((d_own, other, t_y))
    wide = gather(t_y, PLANE)
    near_own = (swap(d_own, y=1), swap(d_own, y=3))
    hidden_other, slope_other = forward(other)
    d_other = backward(d_output[384:], slope_other)
    near_other = (swap(d_other, y=1), swap(d_other, y=3))
    hidden = jnp.concatenate([hidden_own, hidden_other])
    by_z = hidden.reshape(8, 2, 48, 1024)
    mine = pick(by_z, zl, 1).reshape(384, 1024)
    theirs = swap(pick(by_z, 1 - zl, 1).reshape(384, 1024), z=1)

    d_late, near_own = lax.optimization_barrier((d_other, near_own))
    far_own = swap(near_own[1], y=1)
    dt_other = dot(d_late, half, ((1,), (1,))).astype(BF)

    dt_far = swap(dt_other, c=1)
    d_late, wide, near_other, theirs, dt_far = lax.optimization_barrier(
        (d_own, wide, near_other, theirs, dt_far)
    )
    dt = dot(d_late, half, ((1,), (1,))) + dt_far.astype(F32)
    dt = dt.astype(BF)
    d_trunk = lax.psum_scatter(
        dt, AXES, axis_index_groups=PLANE, scatter_dimension=0, tiled=True
    )

    mine, hidden, _ = lax.optimization_barrier((mine, hidden, dt))
    far_other = swap(near_other[0], y=3)
    output = dot(mine, second_own, ((1,), (0,))) + dot(theirs, second_far, ((1,), (0,)))
    output = output.astype(BF).reshape(2, 4, 2, 24, 1024)
    output = jnp.where(c == 0, output, output[::-1])
    output = output.transpose(2, 1, 0, 3, 4).reshape(16, 24, 1024)
    outs = lax.all_to_all(output, "expert", 0, 0, tiled=True)
    wide = after(wide, output)
    wide = wide.reshape(16, 4, 24, 1024).transpose(1, 0, 2, 3).reshape(1536, 1024)
    wide_other = swap(wide, c=1)

    ds = dot(hidden, d_output, ((0,), (0,))).astype(BF)
    ds, outs = lax.optimization_barrier((ds, outs))
    ds = exchange(ds.reshape(4, 256, 1024), RING)
    d_second = jnp.sum(ds, axis=0, dtype=F32).astype(BF)

    mixed = jnp.einsum(
        "etr,ero->rto", gate_rows, outs, preferred_element_type=F32
    ).astype(BF)
    d_gate = jnp.einsum(
        "rto,ero->etr", d_mixed, outs, preferred_element_type=F32
    ).astype(BF)

    d_gate = lax.all_to_all(after(d_gate, ds), "expert", 0, 0, tiled=True)
    d_gate = d_gate.transpose(1, 0, 2).reshape(8, 384)

    tile = dot(wide[:1152], jnp.concatenate([d_own, *near_own]), ((0,), (0,)))
    tile = tile + dot(wide_other[:1152], jnp.concatenate([d_other, *near_other]), ((0,), (0,)))
    tile = tile + dot(wide[1152:], far_own, ((0,), (0,)))
    tile = tile + dot(wide_other[1152:], far_other, ((0,), (0,)))
    tile = tile.astype(BF).reshape(2, 512, 1024)
    far = swap(pick(tile, 1 - zl, 0), z=1)
    near = pick(tile, zl, 0)
    d_first = jnp.where(
        zl == 0,
        jnp.concatenate([near, far], axis=1),
        jnp.concatenate([far, near], axis=1),
    )
    return (mixed, d_trunk, d_gate[None], d_first[None], d_second[None])


def solution(mesh):
    in_specs = (
        P(("dp", "expert"), None),
        P("expert", None, None),
        P("expert", None, None),
        P("expert", None, "dp"),
        P(("dp", "expert"), None, None),
    )
    out_specs = (
        P(("dp", "expert"), None, None),
        P(("dp", "expert"), None),
        P("expert", None, "dp"),
        P("expert", "dp", None),
        P("expert", "dp", None),
    )
    return jax.shard_map(
        on_device, mesh=mesh, in_specs=in_specs, out_specs=out_specs, check_vma=False
    )
```

```python
import jax
import jax.numpy as jnp
from jax import lax
from jax.experimental import pallas as pl
from jax.experimental.pallas import tpu as pltpu
from jax.sharding import PartitionSpec as P

AXES = ("expert", "dp")
BF = jnp.bfloat16
F32 = jnp.float32


def coords(i):
    e, d = divmod(i, 8)
    zl, y = divmod(d, 4)
    zh, r = divmod(e, 8)
    x, c = divmod(r, 2)
    return x, y, zh, zl, c


def index(x, y, zh, zl, c):
    return (zh * 8 + x * 2 + c) * 8 + zl * 4 + y


def swap(v, y=0, z=0, c=0):
    pairs = []
    for i in range(128):
        px, py, pzh, pzl, pc = coords(i)
        pairs.append((i, index(px, py ^ y, pzh ^ (z >> 1), pzl ^ (z & 1), pc ^ c)))
    return lax.ppermute(v, AXES, pairs)


def swap_split(v, k, first):
    pairs = []
    for i in range(128):
        px, py, pzh, pzl, pc = coords(i)
        if (pc == 0) == first:
            pzh, pzl = pzh ^ (k & 1), pzl ^ (k >> 1)
        else:
            px = px ^ k
        pairs.append((i, index(px, py, pzh, pzl, pc)))
    return lax.ppermute(v, AXES, pairs)


def after(v, *others):
    return lax.optimization_barrier((v,) + others)[0]


def grid():
    return [[coords(i), i] for i in range(128)]


def groups(key, order):
    rows = {}
    for at, i in grid():
        rows.setdefault(key(*at), []).append((order(*at), i))
    return [[i for _, i in sorted(rows[k])] for k in sorted(rows)]


PLANE = groups(lambda x, y, zh, zl, c: (y, c), lambda x, y, zh, zl, c: (x, zl, zh))
RING = groups(lambda x, y, zh, zl, c: (x, zh, zl, c), lambda x, y, zh, zl, c: y)


def exchange(v, members):
    return lax.all_to_all(v, AXES, 0, 0, axis_index_groups=members, tiled=True)


def dot(a, b, dims):
    return lax.dot_general(a, b, (dims, ((), ())), preferred_element_type=F32)


def pick(a, i, axis):
    return lax.dynamic_index_in_dim(a, i, axis, keepdims=False)


def gather(v, members):
    return exchange(jnp.broadcast_to(v[None], (len(members[0]),) + v.shape), members)


def place_kernel(at, *refs):
    out = refs[4]
    for i in range(16):
        out[at[i]] = refs[i // 4][i % 4]


def place(kernel, shape, at, lines):
    return pl.pallas_call(
        kernel,
        out_shape=jax.ShapeDtypeStruct(shape, lines[0].dtype),
        in_specs=[pl.BlockSpec(memory_space=pltpu.SMEM)]
        + [pl.BlockSpec(memory_space=pltpu.VMEM)] * 4,
        out_specs=pl.BlockSpec(memory_space=pltpu.VMEM),
        compiler_params=pltpu.CompilerParams(vmem_limit_bytes=16 << 20),
        cost_estimate=pl.CostEstimate(flops=0, bytes_accessed=6 << 20, transcendentals=0),
    )(at, *lines)


def on_device(trunk, w_first, w_second, gates, d_mixed):
    e = lax.axis_index("expert")
    d = lax.axis_index("dp")
    zl, y = d // 4, d % 4
    zh, x, c = e // 8, (e % 8) // 2, e % 2
    zz = zl * 2 + zh

    gate_rows = lax.all_to_all(
        gates[0].reshape(8, 16, 24).transpose(1, 0, 2), "expert", 0, 0, tiled=True
    )

    line = jnp.stack([trunk] + [swap_split(trunk, k, True) for k in (1, 2, 3)])
    far = [swap_split(line, k, False) for k in (2, 1, 3)]
    dx, dz = x ^ (jnp.arange(16) // 4), zz ^ (jnp.arange(16) % 4)
    ex, ez = x ^ (jnp.arange(16) % 4), zz ^ (jnp.arange(16) // 4)
    at = jnp.where(c == 0, dx * 4 + dz, ex * 4 + ez).astype(jnp.int32)
    own = place(place_kernel, (16, 24, 4096), at, [line, far[1], far[0], far[2]])
    own = own.reshape(384, 4096)

    d_out_each = jnp.einsum(
        "etr,rto->ero", after(gate_rows, line), d_mixed, preferred_element_type=F32
    ).astype(BF)
    back = lax.all_to_all(d_out_each, "expert", 0, 0, tiled=True)

    trunk, _ = lax.optimization_barrier((trunk, d_out_each))
    half = lax.dynamic_slice_in_dim(w_first[0], zl * 1024, 1024, 1)
    cols = trunk.reshape(24, 2, 4, 512)
    t_y = [pick(cols, y ^ k, 2).reshape(24, 1024) for k in range(4)]
    t_y = jnp.stack([t_y[0]] + [swap(t_y[k], y=k) for k in (1, 3, 2)])

    own, back, t_y = lax.optimization_barrier((own, back, t_y))
    other = swap(own, c=1)
    back = back.reshape(2, 4, 2, 24, 1024)
    back_z = swap(back, z=1)

    second = w_second[0]
    second_own = lax.dynamic_slice_in_dim(second, zl * 1024, 1024, 0)
    second_far = lax.dynamic_slice_in_dim(second, (1 - zl) * 1024, 1024, 0)

    def forward(rows):
        pre = dot(rows, half, ((1,), (0,)))
        sig = jax.nn.sigmoid(pre)
        slope = sig * (1.0 + pre * (1.0 - sig))
        return (pre * sig).astype(BF), slope

    def backward(d_o, slope):
        d_hidden = dot(d_o, second_own, ((1,), (1,)))
        return (d_hidden * slope).astype(BF)

    hidden_own, slope_own = forward(own)
    hidden_own, back_z = lax.optimization_barrier((hidden_own, back_z))
    pair = jnp.where(zl == 0, jnp.stack([back, back_z]), jnp.stack([back_z, back]))
    pair = pair.transpose(3, 2, 0, 1, 4, 5)
    d_output = jnp.where(c == 0, pair, pair[::-1]).reshape(768, 1024)

    d_own = backward(d_output[:384], slope_own)
    d_own, other, t_y = lax.optimization_barrier((d_own, other, t_y))
    wide = gather(t_y, PLANE)
    near_own = (swap(d_own, y=1), swap(d_own, y=3))
    hidden_other, slope_other = forward(other)
    d_other = backward(d_output[384:], slope_other)
    near_other = (swap(d_other, y=1), swap(d_other, y=3))
    hidden = jnp.concatenate([hidden_own, hidden_other])
    by_z = hidden.reshape(8, 2, 48, 1024)
    mine = pick(by_z, zl, 1).reshape(384, 1024)
    theirs = swap(pick(by_z, 1 - zl, 1).reshape(384, 1024), z=1)

    d_late, near_own = lax.optimization_barrier((d_other, near_own))
    far_own = swap(near_own[1], y=1)
    dt_other = dot(d_late, half, ((1,), (1,))).astype(BF)

    d_late, wide, near_other, dt_other, theirs = lax.optimization_barrier(
        (d_own, wide, near_other, dt_other, theirs)
    )
    dt_far = swap(dt_other, c=1)
    far_other = swap(near_other[0], y=3)

    output = dot(mine, second_own, ((1,), (0,))) + dot(theirs, second_far, ((1,), (0,)))
    output = output.astype(BF).reshape(2, 4, 2, 24, 1024)
    output = jnp.where(c == 0, output, output[::-1])
    output = output.transpose(2, 1, 0, 3, 4).reshape(16, 24, 1024)
    outs = lax.all_to_all(output, "expert", 0, 0, tiled=True)
    d_late, hidden, wide, _ = lax.optimization_barrier((d_late, hidden, wide, output))
    dt = dot(d_late, half, ((1,), (1,))) + dt_far.astype(F32)
    dt, outs = lax.optimization_barrier((dt.astype(BF), outs))
    dt = exchange(dt.reshape(16, 24, 4096), PLANE)
    d_trunk = jnp.sum(dt, axis=0, dtype=F32).astype(BF)
    wide = wide.reshape(16, 4, 24, 1024).transpose(1, 0, 2, 3).reshape(1536, 1024)
    wide_other = swap(wide, c=1)

    ds = dot(hidden, d_output, ((0,), (0,))).astype(BF)
    d_second = lax.psum_scatter(
        ds, AXES, axis_index_groups=RING, scatter_dimension=0, tiled=True
    )

    mixed = jnp.einsum(
        "etr,ero->rto", gate_rows, outs, preferred_element_type=F32
    ).astype(BF)
    d_gate = jnp.einsum(
        "rto,ero->etr", d_mixed, outs, preferred_element_type=F32
    ).astype(BF)

    d_gate = lax.all_to_all(after(d_gate, dt), "expert", 0, 0, tiled=True)
    d_gate = d_gate.transpose(1, 0, 2).reshape(8, 384)

    tile = dot(wide[:1152], jnp.concatenate([d_own, *near_own]), ((0,), (0,)))
    tile = tile + dot(wide_other[:1152], jnp.concatenate([d_other, *near_other]), ((0,), (0,)))
    tile = tile + dot(wide[1152:], far_own, ((0,), (0,)))
    tile = tile + dot(wide_other[1152:], far_other, ((0,), (0,)))
    tile = tile.astype(BF).reshape(2, 512, 1024)
    far = swap(pick(tile, 1 - zl, 0), z=1)
    near = pick(tile, zl, 0)
    d_first = jnp.where(
        zl == 0,
        jnp.concatenate([near, far], axis=1),
        jnp.concatenate([far, near], axis=1),
    )
    return (mixed, d_trunk, d_gate[None], d_first[None], d_second[None])


def solution(mesh):
    in_specs = (
        P(("dp", "expert"), None),
        P("expert", None, None),
        P("expert", None, None),
        P("expert", None, "dp"),
        P(("dp", "expert"), None, None),
    )
    out_specs = (
        P(("dp", "expert"), None, None),
        P(("dp", "expert"), None),
        P("expert", None, "dp"),
        P("expert", "dp", None),
        P("expert", "dp", None),
    )
    return jax.shard_map(
        on_device, mesh=mesh, in_specs=in_specs, out_specs=out_specs, check_vma=False
    )
```

```python
import jax
import jax.numpy as jnp
from jax import lax
from jax.experimental import pallas as pl
from jax.experimental.pallas import tpu as pltpu
from jax.sharding import PartitionSpec as P

AXES = ("expert", "dp")
BF = jnp.bfloat16
F32 = jnp.float32


def coords(i):
    e, d = divmod(i, 8)
    zl, y = divmod(d, 4)
    zh, r = divmod(e, 8)
    x, c = divmod(r, 2)
    return x, y, zh, zl, c


def index(x, y, zh, zl, c):
    return (zh * 8 + x * 2 + c) * 8 + zl * 4 + y


def swap(v, y=0, z=0, c=0):
    pairs = []
    for i in range(128):
        px, py, pzh, pzl, pc = coords(i)
        pairs.append((i, index(px, py ^ y, pzh ^ (z >> 1), pzl ^ (z & 1), pc ^ c)))
    return lax.ppermute(v, AXES, pairs)


def swap_split(v, k, first):
    pairs = []
    for i in range(128):
        px, py, pzh, pzl, pc = coords(i)
        if (pc == 0) == first:
            pzh, pzl = pzh ^ (k & 1), pzl ^ (k >> 1)
        else:
            px = px ^ k
        pairs.append((i, index(px, py, pzh, pzl, pc)))
    return lax.ppermute(v, AXES, pairs)


def after(v, *others):
    return lax.optimization_barrier((v,) + others)[0]


def grid():
    return [[coords(i), i] for i in range(128)]


def groups(key, order):
    rows = {}
    for at, i in grid():
        rows.setdefault(key(*at), []).append((order(*at), i))
    return [[i for _, i in sorted(rows[k])] for k in sorted(rows)]


PLANE = groups(lambda x, y, zh, zl, c: (y, c), lambda x, y, zh, zl, c: (x, zl, zh))
RING = groups(lambda x, y, zh, zl, c: (x, zh, zl, c), lambda x, y, zh, zl, c: y)


def exchange(v, members):
    return lax.all_to_all(v, AXES, 0, 0, axis_index_groups=members, tiled=True)


def dot(a, b, dims):
    return lax.dot_general(a, b, (dims, ((), ())), preferred_element_type=F32)


def pick(a, i, axis):
    return lax.dynamic_index_in_dim(a, i, axis, keepdims=False)


def gather(v, members):
    return exchange(jnp.broadcast_to(v[None], (len(members[0]),) + v.shape), members)


def place_kernel(at, *refs):
    out = refs[4]
    for i in range(16):
        out[at[i]] = refs[i // 4][i % 4]


def take_kernel(at, src, out):
    for i in range(16):
        out[i] = src[at[i]]


def take(at, blocks):
    return pl.pallas_call(
        take_kernel,
        out_shape=jax.ShapeDtypeStruct(blocks.shape, blocks.dtype),
        in_specs=[
            pl.BlockSpec(memory_space=pltpu.SMEM),
            pl.BlockSpec(memory_space=pltpu.VMEM),
        ],
        out_specs=pl.BlockSpec(memory_space=pltpu.VMEM),
        compiler_params=pltpu.CompilerParams(vmem_limit_bytes=16 << 20),
        cost_estimate=pl.CostEstimate(flops=0, bytes_accessed=6 << 20, transcendentals=0),
    )(at, blocks)


def place(kernel, shape, at, lines):
    return pl.pallas_call(
        kernel,
        out_shape=jax.ShapeDtypeStruct(shape, lines[0].dtype),
        in_specs=[pl.BlockSpec(memory_space=pltpu.SMEM)]
        + [pl.BlockSpec(memory_space=pltpu.VMEM)] * 4,
        out_specs=pl.BlockSpec(memory_space=pltpu.VMEM),
        compiler_params=pltpu.CompilerParams(vmem_limit_bytes=16 << 20),
        cost_estimate=pl.CostEstimate(flops=0, bytes_accessed=6 << 20, transcendentals=0),
    )(at, *lines)


def on_device(trunk, w_first, w_second, gates, d_mixed):
    e = lax.axis_index("expert")
    d = lax.axis_index("dp")
    zl, y = d // 4, d % 4
    zh, x, c = e // 8, (e % 8) // 2, e % 2
    zz = zl * 2 + zh

    gate_rows = lax.all_to_all(
        gates[0].reshape(8, 16, 24).transpose(1, 0, 2), "expert", 0, 0, tiled=True
    )

    line = jnp.stack([trunk] + [swap_split(trunk, k, True) for k in (1, 2, 3)])
    far = [swap_split(line, k, False) for k in (2, 1, 3)]
    dx, dz = x ^ (jnp.arange(16) // 4), zz ^ (jnp.arange(16) % 4)
    ex, ez = x ^ (jnp.arange(16) % 4), zz ^ (jnp.arange(16) // 4)
    at = jnp.where(c == 0, dx * 4 + dz, ex * 4 + ez).astype(jnp.int32)
    own = place(place_kernel, (16, 24, 4096), at, [line, far[1], far[0], far[2]])
    own = own.reshape(384, 4096)

    d_out_each = jnp.einsum(
        "etr,rto->ero", after(gate_rows, line), d_mixed, preferred_element_type=F32
    ).astype(BF)
    back = lax.all_to_all(d_out_each, "expert", 0, 0, tiled=True)

    trunk, _ = lax.optimization_barrier((trunk, d_out_each))
    half = lax.dynamic_slice_in_dim(w_first[0], zl * 1024, 1024, 1)
    cols = trunk.reshape(24, 2, 4, 512)
    t_y = [pick(cols, y ^ k, 2).reshape(24, 1024) for k in range(4)]
    t_y = jnp.stack([t_y[0]] + [swap(t_y[k], y=k) for k in (1, 3, 2)])

    own, back, t_y = lax.optimization_barrier((own, back, t_y))
    other = swap(own, c=1)
    back = back.reshape(2, 4, 2, 24, 1024)
    back_z = swap(back, z=1)

    second = w_second[0]
    second_own = lax.dynamic_slice_in_dim(second, zl * 1024, 1024, 0)
    second_far = lax.dynamic_slice_in_dim(second, (1 - zl) * 1024, 1024, 0)

    def forward(rows):
        pre = dot(rows, half, ((1,), (0,)))
        sig = jax.nn.sigmoid(pre)
        slope = sig * (1.0 + pre * (1.0 - sig))
        return (pre * sig).astype(BF), slope

    def backward(d_o, slope):
        d_hidden = dot(d_o, second_own, ((1,), (1,)))
        return (d_hidden * slope).astype(BF)

    hidden_own, slope_own = forward(own)
    hidden_own, back_z = lax.optimization_barrier((hidden_own, back_z))
    pair = jnp.where(zl == 0, jnp.stack([back, back_z]), jnp.stack([back_z, back]))
    pair = pair.transpose(3, 2, 0, 1, 4, 5)
    d_output = jnp.where(c == 0, pair, pair[::-1]).reshape(768, 1024)

    d_own = backward(d_output[:384], slope_own)
    d_own, other, t_y = lax.optimization_barrier((d_own, other, t_y))
    wide = gather(t_y, PLANE)
    near_own = (swap(d_own, y=1), swap(d_own, y=3))
    hidden_other, slope_other = forward(other)
    d_other = backward(d_output[384:], slope_other)
    near_other = (swap(d_other, y=1), swap(d_other, y=3))
    hidden = jnp.concatenate([hidden_own, hidden_other])
    by_z = hidden.reshape(8, 2, 48, 1024)
    mine = pick(by_z, zl, 1).reshape(384, 1024)
    theirs = swap(pick(by_z, 1 - zl, 1).reshape(384, 1024), z=1)

    d_late, near_own = lax.optimization_barrier((d_other, near_own))
    far_own = swap(near_own[1], y=1)
    dt_other = dot(d_late, half, ((1,), (1,))).astype(BF)

    d_late, wide, near_other, dt_other, theirs = lax.optimization_barrier(
        (d_own, wide, near_other, dt_other, theirs)
    )
    dt = dot(d_late, half, ((1,), (1,))) + swap(dt_other, c=1).astype(F32)
    dt = dt.astype(BF)
    far_other = swap(near_other[0], y=3)

    output = dot(mine, second_own, ((1,), (0,))) + dot(theirs, second_far, ((1,), (0,)))
    output = output.astype(BF).reshape(2, 4, 2, 24, 1024)
    output = jnp.where(c == 0, output, output[::-1])
    output = output.transpose(2, 1, 0, 3, 4).reshape(16, 24, 1024)
    output, dt = lax.optimization_barrier((output, dt))
    outs = lax.all_to_all(output, "expert", 0, 0, tiled=True)
    hidden, wide, _ = lax.optimization_barrier((hidden, wide, output))
    dt = take(at, dt.reshape(16, 24, 4096)).reshape(4, 4, 24, 4096)
    total = dt[0].astype(F32)
    for k in (2, 1, 3):
        total = total + swap_split(dt[k], k, False).astype(F32)
    line_dt = total.astype(BF)
    far_other, line_dt = lax.optimization_barrier((far_other, line_dt))
    total = line_dt[0].astype(F32)
    for k in (1, 2, 3):
        total = total + swap_split(line_dt[k], k, True).astype(F32)
    d_trunk = total.astype(BF)
    wide = wide.reshape(16, 4, 24, 1024).transpose(1, 0, 2, 3).reshape(1536, 1024)
    wide_other = swap(wide, c=1)

    ds = dot(hidden, d_output, ((0,), (0,))).astype(BF)
    d_second = lax.psum_scatter(
        ds, AXES, axis_index_groups=RING, scatter_dimension=0, tiled=True
    )

    mixed = jnp.einsum(
        "etr,ero->rto", gate_rows, outs, preferred_element_type=F32
    ).astype(BF)
    d_gate = jnp.einsum(
        "rto,ero->etr", d_mixed, outs, preferred_element_type=F32
    ).astype(BF)

    d_gate = lax.all_to_all(d_gate, "expert", 0, 0, tiled=True)
    d_gate = d_gate.transpose(1, 0, 2).reshape(8, 384)

    tile = dot(wide[:1152], jnp.concatenate([d_own, *near_own]), ((0,), (0,)))
    tile = tile + dot(wide_other[:1152], jnp.concatenate([d_other, *near_other]), ((0,), (0,)))
    tile = tile + dot(wide[1152:], far_own, ((0,), (0,)))
    tile = tile + dot(wide_other[1152:], far_other, ((0,), (0,)))
    tile = tile.astype(BF).reshape(2, 512, 1024)
    far = swap(pick(tile, 1 - zl, 0), z=1)
    near = pick(tile, zl, 0)
    d_first = jnp.where(
        zl == 0,
        jnp.concatenate([near, far], axis=1),
        jnp.concatenate([far, near], axis=1),
    )
    return (mixed, d_trunk, d_gate[None], d_first[None], d_second[None])


def solution(mesh):
    in_specs = (
        P(("dp", "expert"), None),
        P("expert", None, None),
        P("expert", None, None),
        P("expert", None, "dp"),
        P(("dp", "expert"), None, None),
    )
    out_specs = (
        P(("dp", "expert"), None, None),
        P(("dp", "expert"), None),
        P("expert", None, "dp"),
        P("expert", "dp", None),
        P("expert", "dp", None),
    )
    return jax.shard_map(
        on_device, mesh=mesh, in_specs=in_specs, out_specs=out_specs, check_vma=False
    )
```

```python
import jax
import jax.numpy as jnp
from jax import lax
from jax.experimental import pallas as pl
from jax.experimental.pallas import tpu as pltpu
from jax.sharding import PartitionSpec as P

AXES = ("expert", "dp")
BF = jnp.bfloat16
F32 = jnp.float32


def coords(i):
    e, d = divmod(i, 8)
    zl, y = divmod(d, 4)
    zh, r = divmod(e, 8)
    x, c = divmod(r, 2)
    return x, y, zh, zl, c


def index(x, y, zh, zl, c):
    return (zh * 8 + x * 2 + c) * 8 + zl * 4 + y


def swap(v, y=0, z=0, c=0):
    pairs = []
    for i in range(128):
        px, py, pzh, pzl, pc = coords(i)
        pairs.append((i, index(px, py ^ y, pzh ^ (z >> 1), pzl ^ (z & 1), pc ^ c)))
    return lax.ppermute(v, AXES, pairs)


def swap_split(v, k, first):
    pairs = []
    for i in range(128):
        px, py, pzh, pzl, pc = coords(i)
        if (pc == 0) == first:
            pzh, pzl = pzh ^ (k & 1), pzl ^ (k >> 1)
        else:
            px = px ^ k
        pairs.append((i, index(px, py, pzh, pzl, pc)))
    return lax.ppermute(v, AXES, pairs)


def after(v, *others):
    return lax.optimization_barrier((v,) + others)[0]


def grid():
    return [[coords(i), i] for i in range(128)]


def groups(key, order):
    rows = {}
    for at, i in grid():
        rows.setdefault(key(*at), []).append((order(*at), i))
    return [[i for _, i in sorted(rows[k])] for k in sorted(rows)]


PLANE = groups(lambda x, y, zh, zl, c: (y, c), lambda x, y, zh, zl, c: (x, zl, zh))
RING = groups(lambda x, y, zh, zl, c: (x, zh, zl, c), lambda x, y, zh, zl, c: y)


def exchange(v, members):
    return lax.all_to_all(v, AXES, 0, 0, axis_index_groups=members, tiled=True)


def dot(a, b, dims):
    return lax.dot_general(a, b, (dims, ((), ())), preferred_element_type=F32)


def pick(a, i, axis):
    return lax.dynamic_index_in_dim(a, i, axis, keepdims=False)


def gather(v, members):
    return exchange(jnp.broadcast_to(v[None], (len(members[0]),) + v.shape), members)


def place_kernel(at, *refs):
    out = refs[4]
    for k in range(4):
        def step(i, _, k=k):
            out[at[4 * k + i]] = refs[k][i]
            return 0

        lax.fori_loop(0, 4, step, 0)


def take_kernel(at, src, out):
    def step(i, _):
        out[i] = src[at[i]]
        return 0

    lax.fori_loop(0, 16, step, 0)


def take(at, blocks):
    return pl.pallas_call(
        take_kernel,
        out_shape=jax.ShapeDtypeStruct(blocks.shape, blocks.dtype),
        in_specs=[
            pl.BlockSpec(memory_space=pltpu.SMEM),
            pl.BlockSpec(memory_space=pltpu.VMEM),
        ],
        out_specs=pl.BlockSpec(memory_space=pltpu.VMEM),
        compiler_params=pltpu.CompilerParams(vmem_limit_bytes=16 << 20),
        cost_estimate=pl.CostEstimate(flops=0, bytes_accessed=6 << 20, transcendentals=0),
    )(at, blocks)


def place(kernel, shape, at, lines):
    return pl.pallas_call(
        kernel,
        out_shape=jax.ShapeDtypeStruct(shape, lines[0].dtype),
        in_specs=[pl.BlockSpec(memory_space=pltpu.SMEM)]
        + [pl.BlockSpec(memory_space=pltpu.VMEM)] * 4,
        out_specs=pl.BlockSpec(memory_space=pltpu.VMEM),
        compiler_params=pltpu.CompilerParams(vmem_limit_bytes=16 << 20),
        cost_estimate=pl.CostEstimate(flops=0, bytes_accessed=6 << 20, transcendentals=0),
    )(at, *lines)


def on_device(trunk, w_first, w_second, gates, d_mixed):
    e = lax.axis_index("expert")
    d = lax.axis_index("dp")
    zl, y = d // 4, d % 4
    zh, x, c = e // 8, (e % 8) // 2, e % 2
    zz = zl * 2 + zh

    gate_rows = lax.all_to_all(
        gates[0].reshape(8, 16, 24).transpose(1, 0, 2), "expert", 0, 0, tiled=True
    )

    line = jnp.stack([trunk] + [swap_split(trunk, k, True) for k in (1, 2, 3)])
    far = [swap_split(line, k, False) for k in (2, 1, 3)]
    dx, dz = x ^ (jnp.arange(16) // 4), zz ^ (jnp.arange(16) % 4)
    ex, ez = x ^ (jnp.arange(16) % 4), zz ^ (jnp.arange(16) // 4)
    at = jnp.where(c == 0, dx * 4 + dz, ex * 4 + ez).astype(jnp.int32)
    own = place(place_kernel, (16, 24, 4096), at, [line, far[1], far[0], far[2]])
    own = own.reshape(384, 4096)

    d_out_each = jnp.einsum(
        "etr,rto->ero", after(gate_rows, line), d_mixed, preferred_element_type=F32
    ).astype(BF)
    back = lax.all_to_all(d_out_each, "expert", 0, 0, tiled=True)

    trunk, _ = lax.optimization_barrier((trunk, d_out_each))
    half = lax.dynamic_slice_in_dim(w_first[0], zl * 1024, 1024, 1)
    cols = trunk.reshape(24, 2, 4, 512)
    t_y = [pick(cols, y ^ k, 2).reshape(24, 1024) for k in range(4)]
    t_y = jnp.stack([t_y[0]] + [swap(t_y[k], y=k) for k in (1, 3, 2)])

    own, back, t_y = lax.optimization_barrier((own, back, t_y))
    other = swap(own, c=1)
    back = back.reshape(2, 4, 2, 24, 1024)
    back_z = swap(back, z=1)

    second = w_second[0]
    second_own = lax.dynamic_slice_in_dim(second, zl * 1024, 1024, 0)
    second_far = lax.dynamic_slice_in_dim(second, (1 - zl) * 1024, 1024, 0)

    def forward(rows):
        pre = dot(rows, half, ((1,), (0,)))
        sig = jax.nn.sigmoid(pre)
        slope = sig * (1.0 + pre * (1.0 - sig))
        return (pre * sig).astype(BF), slope

    def backward(d_o, slope):
        d_hidden = dot(d_o, second_own, ((1,), (1,)))
        return (d_hidden * slope).astype(BF)

    hidden_own, slope_own = forward(own)
    hidden_own, back_z = lax.optimization_barrier((hidden_own, back_z))
    pair = jnp.where(zl == 0, jnp.stack([back, back_z]), jnp.stack([back_z, back]))
    pair = pair.transpose(3, 2, 0, 1, 4, 5)
    d_output = jnp.where(c == 0, pair, pair[::-1]).reshape(768, 1024)

    d_own = backward(d_output[:384], slope_own)
    d_own, other, t_y = lax.optimization_barrier((d_own, other, t_y))
    wide = gather(t_y, PLANE)
    near_own = (swap(d_own, y=1), swap(d_own, y=3))
    hidden_other, slope_other = forward(other)
    d_other = backward(d_output[384:], slope_other)
    near_other = (swap(d_other, y=1), swap(d_other, y=3))
    hidden = jnp.concatenate([hidden_own, hidden_other])
    by_z = hidden.reshape(8, 2, 48, 1024)
    mine = pick(by_z, zl, 1).reshape(384, 1024)
    theirs = swap(pick(by_z, 1 - zl, 1).reshape(384, 1024), z=1)

    d_late, near_own = lax.optimization_barrier((d_other, near_own))
    far_own = swap(near_own[1], y=1)
    dt_other = dot(d_late, half, ((1,), (1,))).astype(BF)

    d_late, wide, near_other, dt_other, theirs = lax.optimization_barrier(
        (d_own, wide, near_other, dt_other, theirs)
    )
    dt = dot(d_late, half, ((1,), (1,))) + swap(dt_other, c=1).astype(F32)
    dt = dt.astype(BF)
    far_other = swap(near_other[0], y=3)

    output = dot(mine, second_own, ((1,), (0,))) + dot(theirs, second_far, ((1,), (0,)))
    output = output.astype(BF).reshape(2, 4, 2, 24, 1024)
    output = jnp.where(c == 0, output, output[::-1])
    output = output.transpose(2, 1, 0, 3, 4).reshape(16, 24, 1024)
    output, dt = lax.optimization_barrier((output, dt))
    outs = lax.all_to_all(output, "expert", 0, 0, tiled=True)
    hidden, wide, _ = lax.optimization_barrier((hidden, wide, output))
    dt = take(at, dt.reshape(16, 24, 4096)).reshape(4, 4, 24, 4096)
    total = dt[0].astype(F32)
    for k in (2, 1, 3):
        total = total + swap_split(dt[k], k, False).astype(F32)
    line_dt = total.astype(BF)
    far_other, line_dt = lax.optimization_barrier((far_other, line_dt))
    total = line_dt[0].astype(F32)
    for k in (1, 2, 3):
        total = total + swap_split(line_dt[k], k, True).astype(F32)
    d_trunk = total.astype(BF)
    wide = wide.reshape(16, 4, 24, 1024).transpose(1, 0, 2, 3).reshape(1536, 1024)
    wide_other = swap(wide, c=1)

    ds = dot(hidden, d_output, ((0,), (0,))).astype(BF)
    d_second = lax.psum_scatter(
        ds, AXES, axis_index_groups=RING, scatter_dimension=0, tiled=True
    )

    tile = dot(wide, jnp.concatenate([d_own, *near_own, far_own]), ((0,), (0,)))
    tile = tile + dot(
        wide_other, jnp.concatenate([d_other, *near_other, far_other]), ((0,), (0,))
    )
    tile = tile.astype(BF).reshape(2, 512, 1024)
    send, near, outs = lax.optimization_barrier(
        (pick(tile, 1 - zl, 0), pick(tile, zl, 0), outs)
    )
    far = swap(send, z=1)
    mixed = jnp.einsum(
        "etr,ero->rto", gate_rows, outs, preferred_element_type=F32
    ).astype(BF)
    d_gate = jnp.einsum(
        "rto,ero->etr", d_mixed, outs, preferred_element_type=F32
    ).astype(BF)

    d_gate = lax.all_to_all(d_gate, "expert", 0, 0, tiled=True)
    d_gate = d_gate.transpose(1, 0, 2).reshape(8, 384)

    d_first = jnp.where(
        zl == 0,
        jnp.concatenate([near, far], axis=1),
        jnp.concatenate([far, near], axis=1),
    )
    return (mixed, d_trunk, d_gate[None], d_first[None], d_second[None])


def solution(mesh):
    in_specs = (
        P(("dp", "expert"), None),
        P("expert", None, None),
        P("expert", None, None),
        P("expert", None, "dp"),
        P(("dp", "expert"), None, None),
    )
    out_specs = (
        P(("dp", "expert"), None, None),
        P(("dp", "expert"), None),
        P("expert", None, "dp"),
        P("expert", "dp", None),
        P("expert", "dp", None),
    )
    return jax.shard_map(
        on_device, mesh=mesh, in_specs=in_specs, out_specs=out_specs, check_vma=False
    )
```

```python
import jax
import jax.numpy as jnp
from jax import lax
from jax.experimental import pallas as pl
from jax.experimental.pallas import tpu as pltpu
from jax.sharding import PartitionSpec as P

AXES = ("expert", "dp")
BF = jnp.bfloat16
F32 = jnp.float32


def coords(i):
    e, d = divmod(i, 8)
    zl, y = divmod(d, 4)
    zh, r = divmod(e, 8)
    x, c = divmod(r, 2)
    return x, y, zh, zl, c


def index(x, y, zh, zl, c):
    return (zh * 8 + x * 2 + c) * 8 + zl * 4 + y


def swap(v, y=0, z=0, c=0):
    pairs = []
    for i in range(128):
        px, py, pzh, pzl, pc = coords(i)
        pairs.append((i, index(px, py ^ y, pzh ^ (z >> 1), pzl ^ (z & 1), pc ^ c)))
    return lax.ppermute(v, AXES, pairs)


def swap_split(v, k, first):
    pairs = []
    for i in range(128):
        px, py, pzh, pzl, pc = coords(i)
        if (pc == 0) == first:
            pzh, pzl = pzh ^ (k & 1), pzl ^ (k >> 1)
        else:
            px = px ^ k
        pairs.append((i, index(px, py, pzh, pzl, pc)))
    return lax.ppermute(v, AXES, pairs)


def after(v, *others):
    return lax.optimization_barrier((v,) + others)[0]


def grid():
    return [[coords(i), i] for i in range(128)]


def groups(key, order):
    rows = {}
    for at, i in grid():
        rows.setdefault(key(*at), []).append((order(*at), i))
    return [[i for _, i in sorted(rows[k])] for k in sorted(rows)]


PLANE = groups(lambda x, y, zh, zl, c: (y, c), lambda x, y, zh, zl, c: (x, zl, zh))
RING = groups(lambda x, y, zh, zl, c: (x, zh, zl, c), lambda x, y, zh, zl, c: y)


def exchange(v, members):
    return lax.all_to_all(v, AXES, 0, 0, axis_index_groups=members, tiled=True)


def dot(a, b, dims):
    return lax.dot_general(a, b, (dims, ((), ())), preferred_element_type=F32)


def pick(a, i, axis):
    return lax.dynamic_index_in_dim(a, i, axis, keepdims=False)


def gather(v, members):
    return exchange(jnp.broadcast_to(v[None], (len(members[0]),) + v.shape), members)


def place_kernel(at, *refs):
    out = refs[4]
    for k in range(4):
        def step(i, _, k=k):
            out[at[4 * k + i]] = refs[k][i]
            return 0

        lax.fori_loop(0, 4, step, 0)


def take_kernel(at, src, out):
    def step(i, _):
        out[i] = src[at[i]]
        return 0

    lax.fori_loop(0, 16, step, 0)


def take(at, blocks):
    return pl.pallas_call(
        take_kernel,
        out_shape=jax.ShapeDtypeStruct(blocks.shape, blocks.dtype),
        in_specs=[
            pl.BlockSpec(memory_space=pltpu.SMEM),
            pl.BlockSpec(memory_space=pltpu.VMEM),
        ],
        out_specs=pl.BlockSpec(memory_space=pltpu.VMEM),
        compiler_params=pltpu.CompilerParams(vmem_limit_bytes=16 << 20),
        cost_estimate=pl.CostEstimate(flops=0, bytes_accessed=6 << 20, transcendentals=0),
    )(at, blocks)


def place(kernel, shape, at, lines):
    return pl.pallas_call(
        kernel,
        out_shape=jax.ShapeDtypeStruct(shape, lines[0].dtype),
        in_specs=[pl.BlockSpec(memory_space=pltpu.SMEM)]
        + [pl.BlockSpec(memory_space=pltpu.VMEM)] * 4,
        out_specs=pl.BlockSpec(memory_space=pltpu.VMEM),
        compiler_params=pltpu.CompilerParams(vmem_limit_bytes=16 << 20),
        cost_estimate=pl.CostEstimate(flops=0, bytes_accessed=6 << 20, transcendentals=0),
    )(at, *lines)


def on_device(trunk, w_first, w_second, gates, d_mixed):
    e = lax.axis_index("expert")
    d = lax.axis_index("dp")
    zl, y = d // 4, d % 4
    zh, x, c = e // 8, (e % 8) // 2, e % 2
    zz = zl * 2 + zh

    gate_rows = lax.all_to_all(
        gates[0].reshape(8, 16, 24).transpose(1, 0, 2), "expert", 0, 0, tiled=True
    )

    line = jnp.stack([trunk] + [swap_split(trunk, k, True) for k in (1, 2, 3)])
    far = [swap_split(line, k, False) for k in (2, 1, 3)]
    dx, dz = x ^ (jnp.arange(16) // 4), zz ^ (jnp.arange(16) % 4)
    ex, ez = x ^ (jnp.arange(16) % 4), zz ^ (jnp.arange(16) // 4)
    at = jnp.where(c == 0, dx * 4 + dz, ex * 4 + ez).astype(jnp.int32)
    own = place(place_kernel, (16, 24, 4096), at, [line, far[1], far[0], far[2]])
    own = own.reshape(384, 4096)

    d_out_each = jnp.einsum(
        "etr,rto->ero", after(gate_rows, line), d_mixed, preferred_element_type=F32
    ).astype(BF)
    back = lax.all_to_all(d_out_each, "expert", 0, 0, tiled=True)

    trunk, _ = lax.optimization_barrier((trunk, d_out_each))
    half = lax.dynamic_slice_in_dim(w_first[0], zl * 1024, 1024, 1)
    cols = trunk.reshape(24, 2, 4, 512)
    t_y = [pick(cols, y ^ k, 2).reshape(24, 1024) for k in range(4)]
    t_y = jnp.stack([t_y[0]] + [swap(t_y[k], y=k) for k in (1, 3, 2)])

    own, back, t_y = lax.optimization_barrier((own, back, t_y))
    other = swap(own, c=1)
    back = back.reshape(2, 4, 2, 24, 1024)
    back_z = swap(back, z=1)

    second = w_second[0]
    second_own = lax.dynamic_slice_in_dim(second, zl * 1024, 1024, 0)
    second_far = lax.dynamic_slice_in_dim(second, (1 - zl) * 1024, 1024, 0)

    def forward(rows):
        pre = dot(rows, half, ((1,), (0,)))
        sig = jax.nn.sigmoid(pre)
        slope = sig * (1.0 + pre * (1.0 - sig))
        return (pre * sig).astype(BF), slope

    def backward(d_o, slope):
        d_hidden = dot(d_o, second_own, ((1,), (1,)))
        return (d_hidden * slope).astype(BF)

    hidden_own, slope_own = forward(own)
    hidden_own, back_z = lax.optimization_barrier((hidden_own, back_z))
    pair = jnp.where(zl == 0, jnp.stack([back, back_z]), jnp.stack([back_z, back]))
    pair = pair.transpose(3, 2, 0, 1, 4, 5)
    d_output = jnp.where(c == 0, pair, pair[::-1]).reshape(768, 1024)

    d_own = backward(d_output[:384], slope_own)
    d_own, other, t_y = lax.optimization_barrier((d_own, other, t_y))
    wide = gather(t_y, PLANE)
    near_own = (swap(d_own, y=1), swap(d_own, y=3))
    hidden_other, slope_other = forward(other)
    d_other = backward(d_output[384:], slope_other)
    near_other = (swap(d_other, y=1), swap(d_other, y=3))
    hidden = jnp.concatenate([hidden_own, hidden_other])
    by_z = hidden.reshape(8, 2, 48, 1024)
    mine = pick(by_z, zl, 1).reshape(384, 1024)
    theirs = swap(pick(by_z, 1 - zl, 1).reshape(384, 1024), z=1)

    d_late, near_own = lax.optimization_barrier((d_other, near_own))
    far_own = swap(near_own[1], y=1)
    dt_other = dot(d_late, half, ((1,), (1,))).astype(BF)

    d_late, wide, near_other, dt_other, theirs = lax.optimization_barrier(
        (d_own, wide, near_other, dt_other, theirs)
    )
    dt = dot(d_late, half, ((1,), (1,))) + swap(dt_other, c=1).astype(F32)
    dt = dt.astype(BF)
    far_other = swap(near_other[0], y=3)

    output = dot(mine, second_own, ((1,), (0,))) + dot(theirs, second_far, ((1,), (0,)))
    output = output.astype(BF).reshape(2, 4, 2, 24, 1024)
    output = jnp.where(c == 0, output, output[::-1])
    output = output.transpose(2, 1, 0, 3, 4).reshape(16, 24, 1024)
    output, dt = lax.optimization_barrier((output, dt))
    outs = lax.all_to_all(output, "expert", 0, 0, tiled=True)
    hidden, wide, _ = lax.optimization_barrier((hidden, wide, output))
    dt = take(at, dt.reshape(16, 24, 4096)).reshape(4, 4, 24, 4096)
    total = dt[0].astype(F32)
    for k in (2, 1, 3):
        total = total + swap_split(dt[k], k, False).astype(F32)
    line_dt = total.astype(BF)
    far_other, line_dt = lax.optimization_barrier((far_other, line_dt))
    total = line_dt[0].astype(F32)
    for k in (1, 2, 3):
        total = total + swap_split(line_dt[k], k, True).astype(F32)
    d_trunk = total.astype(BF)
    wide = wide.reshape(16, 4, 24, 1024).transpose(1, 0, 2, 3).reshape(1536, 1024)
    wide_other = swap(wide, c=1)

    ds = dot(hidden, d_output, ((0,), (0,))).astype(BF)
    d_second = lax.psum_scatter(
        ds, AXES, axis_index_groups=RING, scatter_dimension=0, tiled=True
    )

    mixed = jnp.einsum(
        "etr,ero->rto", gate_rows, outs, preferred_element_type=F32
    ).astype(BF)
    d_gate = jnp.einsum(
        "rto,ero->etr", d_mixed, outs, preferred_element_type=F32
    ).astype(BF)

    d_gate = lax.all_to_all(d_gate, "expert", 0, 0, tiled=True)
    d_gate = d_gate.transpose(1, 0, 2).reshape(8, 384)

    tile = dot(wide[:1152], jnp.concatenate([d_own, *near_own]), ((0,), (0,)))
    tile = tile + dot(wide_other[:1152], jnp.concatenate([d_other, *near_other]), ((0,), (0,)))
    tile = tile + dot(
        jnp.concatenate([wide[1152:], wide_other[1152:]]),
        jnp.concatenate([far_own, far_other]),
        ((0,), (0,)),
    )
    tile = tile.astype(BF).reshape(2, 512, 1024)
    far = swap(pick(tile, 1 - zl, 0), z=1)
    near = pick(tile, zl, 0)
    d_first = jnp.where(
        zl == 0,
        jnp.concatenate([near, far], axis=1),
        jnp.concatenate([far, near], axis=1),
    )
    return (mixed, d_trunk, d_gate[None], d_first[None], d_second[None])


def solution(mesh):
    in_specs = (
        P(("dp", "expert"), None),
        P("expert", None, None),
        P("expert", None, None),
        P("expert", None, "dp"),
        P(("dp", "expert"), None, None),
    )
    out_specs = (
        P(("dp", "expert"), None, None),
        P(("dp", "expert"), None),
        P("expert", None, "dp"),
        P("expert", "dp", None),
        P("expert", "dp", None),
    )
    return jax.shard_map(
        on_device, mesh=mesh, in_specs=in_specs, out_specs=out_specs, check_vma=False
    )
```
